32 devices in a mesh: groups: 2 (over x), tm: 16 (over z, y, core).
Axes of the slice: x: 2, y: 2, z: 4, core: 2. Of those that a mesh axis runs over, the one named last changes fastest.
Arguments:
- features: bfloat16 [32768, 80], P(('groups', 'tm')), parts along dimension 0, may hold values from -6 to 6
- stem_kernel: bfloat16 [3, 3, 256], replicated, may hold values from -3 to 3
- mid_depthwise: bfloat16 [3, 3, 256], replicated, may hold values from -3 to 3
- mid_pointwise: bfloat16 [256, 256], replicated, may hold values from -0.5 to 0.5
- last_depthwise: bfloat16 [3, 3, 256], replicated, may hold values from -3 to 3
- last_pointwise: bfloat16 [256, 256], replicated, may hold values from -0.5 to 0.5
- proj_weight: bfloat16 [2560, 1024], replicated, may hold values from -0.15625 to 0.15625
- norm_gain: float32 [1024], replicated, may hold values from 0.25 to 1.75
- qkv_weight: bfloat16 [1024, 3072], replicated
- out_weight: bfloat16 [1024, 1024], replicated, may hold values from -0.1875 to 0.1875
- cotangent: bfloat16 [4096, 1024], P(('groups', 'tm')), parts along dimension 0, may hold values from -6 to 6
- utt_bounds: int32 [16, 2], P('groups'), parts along dimension 0, may hold values from 0 to 2048, as said below
- live_blocks: int32 [32, 7], P(('groups', 'tm')), parts along dimension 0, may hold values from 0 to 1, as said below
Outputs:
- block_out: bfloat16 [4096, 1024], P(('groups', 'tm')), parts along dimension 0
- frame_grads: bfloat16 [4096, 1024], P(('groups', 'tm')), parts along dimension 0
- proj_grads: float32 [5120, 1024], P(('groups', 'tm')), parts along dimension 0
The draws below stay inside these ranges and needn't reach their ends.
There are 2 independent parts, one for each index of `groups`. The reference program is written for one: setup_inputs(seed, part) draws one part's arguments, and reference() takes and returns one part's arrays. A program takes and returns all parts, laid end to end along the dimension named above; an argument that names none is the same for every part. Nothing has to cross between parts.
Inputs may be any that keep to these rules, and one draw needn't show every extreme that they name: `utt_bounds`: rows are in order of time and tile frames 0 to 2048 without gaps; each utterance has 1 to 384 frames and one has exactly 384. `live_blocks`: entry [b, c] is 1 iff some utterance has frames in block b (frames b * 128 to (b + 1) * 128 - 1) and in block b + c - 3; it is 0 where that block lies outside the recording.
All inputs are finite; a program needn't handle non-finite values.
Results may differ from the reference program's by a relative error of at most 0.015.
Values may be sent and summed in bfloat16 or wider, within the bound.
A program may use at most 128 MiB of HBM per device.

```python
import math
import jax
import jax.numpy as jnp
from jax import lax

D = 1024
HEADS = 8
CHANNELS = 256
MEL = 80
FRAME_DEV = 128
REACH = 3
HEAD_DIM = 128
PROJ_IN = 2560
FRAMES = 2048
FEAT_ROWS = 16384
MAXLEN = 384
UTTS = 8


def utterance_bounds(key):
    base_key = jax.random.fold_in(key, 7)
    order_key, weight_key = jax.random.split(base_key)
    spare_frames = FRAMES - UTTS
    full_count = spare_frames // (MAXLEN - 1)
    short_count = UTTS - full_count
    remaining = spare_frames - full_count * (MAXLEN - 1)
    weights = jax.random.randint(weight_key, (short_count,), 32, 64)
    extra_frames = remaining * weights // jnp.sum(weights)
    leftover = remaining - jnp.sum(extra_frames)
    positions = jnp.arange(short_count)
    short_lengths = 1 + extra_frames + (positions < leftover).astype(jnp.int32)
    full_lengths = jnp.full((full_count,), MAXLEN, jnp.int32)
    all_lengths = jnp.concatenate([full_lengths, short_lengths.astype(jnp.int32)])
    order = jax.random.permutation(order_key, UTTS)
    lengths = all_lengths[order]
    utt_ends = jnp.cumsum(lengths)
    starts = utt_ends - lengths
    return jnp.stack([starts, utt_ends], axis=1).astype(jnp.int32)


def segment_at(positions, bounds):
    return jnp.sum((bounds[None, :, 0] <= positions[:, None]).astype(jnp.int32), axis=1) - 1


def draw_utt_bounds(key, part):
    return utterance_bounds(key)


def draw_live_blocks(key, part):
    bounds = utterance_bounds(key)
    blocks = FRAMES // FRAME_DEV
    firsts = jnp.arange(blocks) * FRAME_DEV
    block_lasts = firsts + FRAME_DEV - 1
    seg_first = segment_at(firsts, bounds)
    seg_last = segment_at(block_lasts, bounds)
    offsets = jnp.arange(2 * REACH + 1) - REACH
    partner = jnp.arange(blocks)[:, None] + offsets[None, :]
    inside = (partner >= 0) & (partner < blocks)
    clipped = jnp.clip(partner, 0, blocks - 1)
    forward_share = seg_last[:, None] == seg_first[clipped]
    earlier = seg_first[:, None] == seg_last[clipped]
    shared = jnp.where(offsets[None, :] > 0, forward_share, jnp.where(offsets[None, :] < 0, earlier, True)) & inside
    return shared.astype(jnp.int32)


def draw_qkv_weight(key, part):
    weights = jax.random.normal(jax.random.fold_in(key, 11), (D, 3 * D), jnp.float32) / math.sqrt(D)
    head_factor = jax.random.uniform(jax.random.fold_in(key, 13), (HEADS,), jnp.float32, 2.0, 3.5)
    column = jnp.arange(D)
    head_of = column // HEAD_DIM
    column_factor = head_factor[head_of]
    query_part = weights[:, :D] * column_factor[None, :]
    return jnp.concatenate([query_part, weights[:, D:]], axis=1).astype(jnp.bfloat16)


def block_levels(rng, shape, cuts, least, top_value):
    loudness = 1.0
    for dim, blocks in cuts:
        heights = jax.random.uniform(jax.random.fold_in(jax.random.fold_in(rng, 6), dim), (blocks,), jnp.float32, least / len(cuts), top_value / len(cuts))
        loudness = loudness * jnp.repeat(jnp.exp(heights), shape[dim] // blocks).reshape((-1,) + (1,) * (len(shape) - 1 - dim))
    return loudness


def gaussian(own_key, extent, width, most, pieces=(), kind=jnp.bfloat16):
    loudness = block_levels(own_key, extent, pieces, -0.22, 0.18) if pieces else 1.0
    entries = jax.random.normal(own_key, extent, jnp.float32) * width * loudness
    return jnp.minimum(jnp.maximum(entries, -most), most).astype(kind)


def setup_inputs(seed: int = 0, part: int = 0) -> dict:
    seeds = jax.random.split(jax.random.key(seed), 14)
    part_splits = jax.random.split(jax.random.fold_in(seeds[13], part), 14)
    return {
        "features": gaussian(part_splits[0], (FEAT_ROWS, MEL), 1.0, 6.0, ((0, 16),)),
        "stem_kernel": gaussian(seeds[1], (3, 3, CHANNELS), 4 ** -0.5, 3.0),
        "mid_depthwise": gaussian(seeds[2], (3, 3, CHANNELS), 4 ** -0.5, 3.0),
        "mid_pointwise": gaussian(seeds[3], (CHANNELS, CHANNELS), (CHANNELS // 2) ** -0.5, 0.5),
        "last_depthwise": gaussian(seeds[4], (3, 3, CHANNELS), 4 ** -0.5, 3.0),
        "last_pointwise": gaussian(seeds[5], (CHANNELS, CHANNELS), (CHANNELS // 2) ** -0.5, 0.5),
        "proj_weight": gaussian(seeds[6], (PROJ_IN, D), (PROJ_IN // 2) ** -0.5, 0.15625),
        "norm_gain": jnp.clip(1.0 + 0.15 * jax.random.normal(seeds[7], (D,), jnp.float32), 0.25, 1.75),
        "qkv_weight": draw_qkv_weight(jax.random.fold_in(seeds[13], 71), part),
        "out_weight": gaussian(seeds[9], (D, D), D ** -0.5, 0.1875),
        "cotangent": gaussian(part_splits[10], (FRAMES, D), 1.0, 6.0, ((0, 16),)),
        "utt_bounds": draw_utt_bounds(jax.random.fold_in(jax.random.fold_in(seeds[13], part), 71), part),
        "live_blocks": draw_live_blocks(jax.random.fold_in(jax.random.fold_in(seeds[13], part), 71), part),
    }


norm_eps = 1e-05
neg_fill = -1e+30

def rounded(values):
    return lax.optimization_barrier(values.astype(jnp.bfloat16)).astype(jnp.float32)

def conv_same(inputs, kernel, groups):
    result = lax.conv_general_dilated(inputs[None], kernel, (2, 2), ((1, 1), (1, 1)), dimension_numbers=('NHWC', 'HWIO', 'NHWC'), feature_group_count=groups, preferred_element_type=jnp.float32)
    return result[0]

def pointwise(depth_out, weight):
    in_shape = depth_out.shape
    mixed_rows = jnp.dot(depth_out.reshape(-1, in_shape[-1]), weight, preferred_element_type=jnp.float32)
    return jax.nn.relu(mixed_rows).reshape(in_shape[:-1] + (weight.shape[1],)).astype(jnp.bfloat16)

def segment_of(positions, utt_bounds):
    inside = (utt_bounds[None, :, 0] <= positions[:, None]) & (positions[:, None] < utt_bounds[None, :, 1])
    number = jnp.arange(utt_bounds.shape[0], dtype=jnp.int32)
    found = lax.optimization_barrier(jnp.sum(jnp.where(inside, number[None, :], 0), axis=1)).astype(jnp.int32)
    return jnp.where(jnp.any(inside, axis=1), found, -1).astype(jnp.int32)

def reference(features, stem_kernel, mid_depthwise, mid_pointwise, last_depthwise, last_pointwise, proj_weight, norm_gain, qkv_weight, out_weight, cotangent, utt_bounds, live_blocks):
    channels = stem_kernel.shape[-1]
    first_section = jax.nn.relu(conv_same(features[:, :, None], stem_kernel[:, :, None, :], 1)).astype(jnp.bfloat16)
    mid_depth = conv_same(first_section, mid_depthwise[:, :, None, :], channels).astype(jnp.bfloat16)
    second_section = pointwise(mid_depth, mid_pointwise)
    last_depth = conv_same(second_section, last_depthwise[:, :, None, :], channels).astype(jnp.bfloat16)
    third_section = pointwise(last_depth, last_pointwise)
    flat_rows = third_section.reshape(FRAMES, PROJ_IN)
    frames = jnp.dot(flat_rows, proj_weight, preferred_element_type=jnp.float32).astype(jnp.bfloat16)
    frames_f = frames.astype(jnp.float32)
    row_mean = lax.optimization_barrier(jnp.mean(frames_f, axis=-1, keepdims=True))
    centered = frames_f - row_mean
    inv_std = lax.rsqrt(lax.optimization_barrier(jnp.mean(centered * centered, axis=-1, keepdims=True)) + norm_eps)
    normalized = centered * inv_std
    normed = (normalized * norm_gain.astype(jnp.float32)).astype(jnp.bfloat16)
    projected = jnp.dot(normed, qkv_weight, preferred_element_type=jnp.float32).astype(jnp.bfloat16)
    score_scale = HEAD_DIM ** (-0.5)
    query_heads = projected[:, :D].astype(jnp.float32).reshape(FRAMES, HEADS, HEAD_DIM)
    key_pad = jnp.pad(projected[:, D:2 * D].astype(jnp.float32), ((MAXLEN, MAXLEN), (0, 0))).reshape(-1, HEADS, HEAD_DIM)
    value_pad = jnp.pad(projected[:, 2 * D:].astype(jnp.float32), ((MAXLEN, MAXLEN), (0, 0))).reshape(-1, HEADS, HEAD_DIM)
    segments = segment_of(jnp.arange(FRAMES, dtype=jnp.int32), utt_bounds)
    segment_pad = jnp.pad(segments, (MAXLEN, MAXLEN), constant_values=-1)
    query_block = math.gcd(FRAMES, 512)
    key_window = query_block + 2 * MAXLEN
    block_starts = jnp.arange(FRAMES // query_block, dtype=jnp.int32) * query_block

    def window_scores(row_start):
        query_pos = row_start + jnp.arange(query_block, dtype=jnp.int32)
        key_pos = row_start - MAXLEN + jnp.arange(key_window, dtype=jnp.int32)
        query_seg = lax.dynamic_slice_in_dim(segments, row_start, query_block)
        key_seg = lax.dynamic_slice_in_dim(segment_pad, row_start, key_window)
        query_blk = query_pos // FRAME_DEV
        offsets = ((key_pos + MAXLEN) // FRAME_DEV - REACH)[None, :] - query_blk[:, None]
        block_flags = live_blocks[query_blk[:, None], jnp.clip(offsets + REACH, 0, 2 * REACH)]
        allowed = (query_seg[:, None] == key_seg[None, :]) & (jnp.abs(offsets) <= REACH) & (block_flags == 1)
        query_part = lax.dynamic_slice_in_dim(query_heads, row_start, query_block)
        key_part = lax.dynamic_slice_in_dim(key_pad, row_start, key_window)
        value_part = lax.dynamic_slice_in_dim(value_pad, row_start, key_window)
        scores = jnp.einsum('qhd,khd->hqk', query_part, key_part) * score_scale
        return (jnp.where(allowed[None], scores, neg_fill), query_part, key_part, value_part)

    def forward_block(row_start):
        scores, query_part, key_part, value_part = window_scores(row_start)
        row_max = lax.optimization_barrier(jnp.max(scores, axis=-1))
        log_norm = row_max + jnp.log(lax.optimization_barrier(jnp.sum(jnp.exp(scores - row_max[..., None]), axis=-1)))
        probs = rounded(jnp.exp(scores - log_norm[..., None]))
        mixed_heads = jnp.einsum('hqk,khd->qhd', probs, value_part)
        return (mixed_heads.reshape(query_block, D).astype(jnp.bfloat16), log_norm)
    attention_blocks, log_norms = lax.map(forward_block, block_starts)
    attention = attention_blocks.reshape(FRAMES, D)
    block_out = (frames_f + jnp.dot(attention, out_weight, preferred_element_type=jnp.float32)).astype(jnp.bfloat16)
    d_attention = jnp.dot(cotangent, out_weight.T, preferred_element_type=jnp.float32).astype(jnp.bfloat16)
    d_heads = d_attention.astype(jnp.float32).reshape(FRAMES, HEADS, HEAD_DIM)
    delta = lax.optimization_barrier(jnp.sum(d_heads * attention.astype(jnp.float32).reshape(FRAMES, HEADS, HEAD_DIM), axis=-1))

    def backward_block(carried, inputs_now):
        row_start, log_norm = inputs_now
        scores, query_part, key_part, value_part = window_scores(row_start)
        dout_part = lax.dynamic_slice_in_dim(d_heads, row_start, query_block)
        delta_part = lax.dynamic_slice_in_dim(delta, row_start, query_block).T
        weights_full = jnp.exp(scores - log_norm[..., None])
        dprob = jnp.einsum('qhd,khd->hqk', dout_part, value_part)
        dscore = rounded(weights_full * (dprob - delta_part[..., None]))
        grad_rows = (score_scale * jnp.einsum('hqk,khd->qhd', dscore, key_part)).reshape(query_block, D).astype(jnp.bfloat16)
        grad_keys = score_scale * jnp.einsum('hqk,qhd->khd', dscore, query_part)
        grad_values = jnp.einsum('hqk,qhd->khd', rounded(weights_full), dout_part)
        both_grads = jnp.stack([grad_keys, grad_values]).reshape(2, key_window, D)
        current = lax.dynamic_slice_in_dim(carried, row_start, key_window, axis=1)
        carried = lax.dynamic_update_slice_in_dim(carried, current + both_grads, row_start, axis=1)
        return (carried, grad_rows)
    start_sums = jnp.zeros((2, FRAMES + 2 * MAXLEN, D), jnp.float32)
    key_sums, grad_blocks = lax.scan(backward_block, start_sums, (block_starts, log_norms))
    grad_query = grad_blocks.reshape(FRAMES, D)
    grad_key = key_sums[0, MAXLEN:MAXLEN + FRAMES].astype(jnp.bfloat16)
    grad_value = key_sums[1, MAXLEN:MAXLEN + FRAMES].astype(jnp.bfloat16)
    grad_normed = jnp.dot(jnp.concatenate([grad_query, grad_key, grad_value], axis=1), qkv_weight.T, preferred_element_type=jnp.float32)
    scaled_grad = grad_normed * norm_gain.astype(jnp.float32)
    ln_grad = inv_std * (scaled_grad - lax.optimization_barrier(jnp.mean(scaled_grad, axis=-1, keepdims=True)) - normalized * lax.optimization_barrier(jnp.mean(scaled_grad * normalized, axis=-1, keepdims=True)))
    frame_grads = (cotangent.astype(jnp.float32) + ln_grad).astype(jnp.bfloat16)
    proj_grads = jnp.dot(flat_rows.T, frame_grads, preferred_element_type=jnp.float32)
    return (block_out, frame_grads, proj_grads)
```

```python
import functools

import jax
import jax.numpy as jnp
from jax import lax
from jax.experimental import pallas as pl
from jax.experimental.pallas import tpu as pltpu
from jax.sharding import PartitionSpec as P

HEADS = 8
REACH = 3
HEAD_DIM = 128
norm_eps = 1e-05
neg_fill = -1e30
MEL_PITCH = 84
SCALE = HEAD_DIM ** (-0.5)


def dot_nt(a, b):
    return lax.dot_general(a, b, (((1,), (1,)), ((), ())), preferred_element_type=jnp.float32)


def dot_tn(a, b):
    return lax.dot_general(a, b, (((0,), (0,)), ((), ())), preferred_element_type=jnp.float32)


def dot_nn(a, b):
    return jnp.dot(a, b, preferred_element_type=jnp.float32)


def subsample_kernel(
    x_ref, stem_ref, mid_dw_ref, mid_pw_ref, last_dw_ref, last_pw_ref, flat_ref, even, odd, second, shifted
):
    rows = x_ref.shape[0] // 4
    main = rows - 8
    mids = second.shape[0] - 1
    span = shifted.shape[1] - 256
    odd[0] = jnp.zeros(odd.shape[1:], odd.dtype)
    second[0] = jnp.zeros(second.shape[1:], second.dtype)
    for i in range(4):
        shifted[i] = stem_ref[8 - 2 * i : 8 - 2 * i + span + 256, :]

    def step(k, half):
        def stem(i):
            start = pl.multiple_of(span - 8 * k, 8)
            taps = shifted[i, pl.ds(start, 256), :].astype(jnp.bfloat16)
            return jnp.maximum(dot_nn(x_ref[...], taps), 0.0).reshape(even.shape)

        m = 2 * k + half
        even[...] = stem(2 * half)
        odd[1 - half] = stem(2 * half + 1)
        parts = (odd.at[half], even, odd.at[1 - half])
        early = jnp.zeros((main, 256), jnp.float32)
        late = jnp.zeros((rows, 256), jnp.float32)
        for df in range(3):
            src = parts[df]
            for dt in range(3):
                tap = mid_dw_ref[3 * dt + df : 3 * dt + df + 1, :]
                phase = (3, 0, 1)[dt]
                start = 7 if dt == 0 else 8
                early += src[phase, start : start + main, :] * tap
                late += src[dt + 1] * tap
        weight = mid_pw_ref[...]
        second[m + 1, 0, 8:rows, :] = jnp.maximum(dot_nn(early.astype(jnp.bfloat16), weight), 0.0)
        second[m + 1, 1] = jnp.maximum(dot_nn(late.astype(jnp.bfloat16), weight), 0.0)

    def body(k, _):
        step(k, 0)
        step(k, 1)
        return 0

    lax.fori_loop(0, mids // 2, body, 0)
    for f in range(mids // 2):
        total = jnp.zeros((main, 256), jnp.float32)
        for df in range(3):
            for dt in range(3):
                tap = last_dw_ref[3 * dt + df : 3 * dt + df + 1, :]
                phase = (1, 0, 1)[dt]
                start = 7 if dt == 0 else 8
                total += second[2 * f + df, phase, start : start + main, :] * tap
        out = jnp.maximum(dot_nn(total.astype(jnp.bfloat16), last_pw_ref[...]), 0.0)
        flat_ref[:, f * 256 : (f + 1) * 256] = out.astype(jnp.bfloat16)


def subsample(features, halo, stem_kernel, mid_depthwise, mid_pointwise, last_depthwise, last_pointwise):
    feat_rows, mel = features.shape
    main = feat_rows // 8
    rows = main + 8
    channels = stem_kernel.shape[-1]
    mids = mel // 4
    series = jnp.concatenate([jnp.zeros((56, mel), features.dtype), halo, features], axis=0)
    series = jnp.pad(series, ((0, 0), (1, MEL_PITCH - mel - 1)))
    late = jnp.pad(series, ((1, 0), (0, 0)))[:-1].reshape(rows, 8 * MEL_PITCH)
    tail = series.reshape(rows, 8 * MEL_PITCH)[:, 7 * MEL_PITCH :]
    wide = jnp.concatenate([late, tail], axis=1)
    x = jnp.concatenate(
        [wide[:, 2 * p * MEL_PITCH : (2 * p + 3) * MEL_PITCH] for p in range(4)], axis=0
    )
    x = jnp.pad(x, ((0, 0), (0, 256 - 3 * MEL_PITCH)))
    base = jnp.pad(stem_kernel.astype(jnp.float32), ((0, 0), (0, MEL_PITCH - 3), (0, 0)))
    base = base.reshape(3 * MEL_PITCH, channels)
    base = jnp.pad(base, ((mel + 8, 256 - 3 * MEL_PITCH), (0, 0)))
    return pl.pallas_call(
        subsample_kernel,
        out_shape=jax.ShapeDtypeStruct((main, (mids // 2) * channels), jnp.bfloat16),
        in_specs=[pl.BlockSpec(memory_space=pltpu.VMEM)] * 6,
        out_specs=pl.BlockSpec(memory_space=pltpu.VMEM),
        scratch_shapes=[
            pltpu.VMEM((4, rows, channels), jnp.float32),
            pltpu.VMEM((2, 4, rows, channels), jnp.float32),
            pltpu.VMEM((mids + 1, 2, rows, channels), jnp.float32),
            pltpu.VMEM((4, mel + 256, channels), jnp.float32),
        ],
        compiler_params=pltpu.CompilerParams(vmem_limit_bytes=40 * 1024 * 1024),
        cost_estimate=pl.CostEstimate(
            flops=20_000_000_000, bytes_accessed=2_000_000, transcendentals=0
        ),
        name="subsample",
    )(
        x,
        base,
        mid_depthwise.reshape(9, channels).astype(jnp.float32),
        mid_pointwise,
        last_depthwise.reshape(9, channels).astype(jnp.float32),
        last_pointwise,
    )


def forward_kernel(own, q_ref, k_ref, v_ref, do_ref, bias_ref, out_ref, stat_ref):
    scores = dot_nt(k_ref[...], q_ref[...]) * SCALE + bias_ref[...]
    top = jnp.max(scores, axis=0, keepdims=True)
    weights = jnp.exp(scores - top)
    total = jnp.sum(weights, axis=0, keepdims=True)
    probs = (weights / total).astype(jnp.bfloat16)
    out = dot_tn(probs, v_ref[...])
    out_ref[...] = out.astype(jnp.bfloat16)
    stat_ref[0, 0:1, :] = top + jnp.log(total)
    prod = do_ref[...].astype(jnp.float32) * out
    stat_ref[0, 1:2, :] = jnp.sum(prod.T, axis=0, keepdims=True)


def backward_kernel(own, q_ref, k_ref, v_ref, do_ref, stat_ref, bias_ref, bias2_ref, dq_ref, dk_ref, dv_ref):
    rows = own.stop - own.start
    blocks = q_ref.shape[0] // rows
    q_own, k_own, v_own, do_own = (r[own, :] for r in (q_ref, k_ref, v_ref, do_ref))
    mid = blocks // 2
    log_norm = stat_ref[mid, 0, 0:1, :]
    delta = stat_ref[mid, 0, 1:2, :]
    weights = jnp.exp(dot_nt(k_ref[...], q_own) * SCALE + bias_ref[...] - log_norm)
    dscore = (weights * (dot_nt(v_ref[...], do_own) - delta)).astype(jnp.bfloat16)
    dq_ref[...] = (dot_tn(dscore, k_ref[...]) * SCALE).astype(jnp.bfloat16)
    log_norms = jnp.concatenate([stat_ref[b, 0, 0:1, :] for b in range(blocks)], axis=1)
    deltas = jnp.concatenate([stat_ref[b, 0, 1:2, :] for b in range(blocks)], axis=1)
    weights2 = jnp.exp(dot_nt(k_own, q_ref[...]) * SCALE + bias2_ref[...] - log_norms)
    dscore2 = (weights2 * (dot_nt(v_own, do_ref[...]) - deltas)).astype(jnp.bfloat16)
    dk_ref[...] = (dot_nn(dscore2, q_ref[...]) * SCALE).astype(jnp.bfloat16)
    dv_ref[...] = dot_nn(weights2.astype(jnp.bfloat16), do_ref[...]).astype(jnp.bfloat16)


def attention_forward(projected, d_attention, bias, rows):
    window = projected.shape[0]
    width = HEADS * HEAD_DIM
    own = slice(REACH * rows, (REACH + 1) * rows)
    return pl.pallas_call(
        functools.partial(forward_kernel, own),
        grid=(HEADS,),
        out_shape=(
            jax.ShapeDtypeStruct((rows, width), jnp.bfloat16),
            jax.ShapeDtypeStruct((HEADS, 2, rows), jnp.float32),
        ),
        in_specs=[
            pl.BlockSpec((rows, HEAD_DIM), lambda h: (REACH, h)),
            pl.BlockSpec((window, HEAD_DIM), lambda h: (0, HEADS + h)),
            pl.BlockSpec((window, HEAD_DIM), lambda h: (0, 2 * HEADS + h)),
            pl.BlockSpec((rows, HEAD_DIM), lambda h: (REACH, h)),
            pl.BlockSpec((window, rows), lambda h: (0, 0)),
        ],
        out_specs=(
            pl.BlockSpec((rows, HEAD_DIM), lambda h: (0, h)),
            pl.BlockSpec((1, 2, rows), lambda h: (h, 0, 0)),
        ),
        name="attention_forward",
    )(projected, projected, projected, d_attention, bias)


def attention_backward(projected, d_attention, stats, bias, bias2, rows):
    window = projected.shape[0]
    width = HEADS * HEAD_DIM
    own = slice(REACH * rows, (REACH + 1) * rows)
    grad = jax.ShapeDtypeStruct((rows, width), jnp.bfloat16)
    return pl.pallas_call(
        functools.partial(backward_kernel, own),
        grid=(HEADS,),
        out_shape=(grad, grad, grad),
        in_specs=[
            pl.BlockSpec((window, HEAD_DIM), lambda h: (0, h)),
            pl.BlockSpec((window, HEAD_DIM), lambda h: (0, HEADS + h)),
            pl.BlockSpec((window, HEAD_DIM), lambda h: (0, 2 * HEADS + h)),
            pl.BlockSpec((window, HEAD_DIM), lambda h: (0, h)),
            pl.BlockSpec((2 * REACH + 1, 1, 2, rows), lambda h: (0, h, 0, 0)),
            pl.BlockSpec((window, rows), lambda h: (0, 0)),
            pl.BlockSpec((rows, window), lambda h: (0, 0)),
        ],
        out_specs=(pl.BlockSpec((rows, HEAD_DIM), lambda h: (0, h)),) * 3,
        name="attention_backward",
    )(projected, projected, projected, d_attention, stats, bias, bias2)


def gathered_window(x, size):
    def moved(value, pairs):
        return lax.ppermute(value, "tm", pairs)

    swap = [(i, i ^ 1) for i in range(size)]
    before = moved(x, [(i, i + 2) for i in range(size - 2)])
    after = moved(x, [(i, i - 2) for i in range(2, size)])
    far = [(i, i + 3) for i in range(1, size, 2) if i + 3 < size]
    far += [(i, i - 3) for i in range(0, size, 2) if i - 3 >= 0]
    far_block = moved(x, far)
    sibling = moved(x, swap)
    sib_before = moved(before, swap)
    sib_after = moved(after, swap)
    is_even = lax.axis_index("tm") % 2 == 0

    def pick(a, b):
        return jnp.where(is_even, a, b)

    return [
        pick(far_block, sib_before),
        before,
        pick(sib_before, sibling),
        x,
        pick(sibling, sib_after),
        after,
        pick(sib_after, far_block),
    ]


def segment_of(positions, utt_bounds):
    inside = (utt_bounds[None, :, 0] <= positions[:, None]) & (
        positions[:, None] < utt_bounds[None, :, 1]
    )
    number = jnp.arange(utt_bounds.shape[0], dtype=jnp.int32)
    found = jnp.sum(jnp.where(inside, number[None, :], 0), axis=1)
    return jnp.where(jnp.any(inside, axis=1), found, -1)


def per_device(
    size,
    features,
    stem_kernel,
    mid_depthwise,
    mid_pointwise,
    last_depthwise,
    last_pointwise,
    proj_weight,
    norm_gain,
    qkv_weight,
    out_weight,
    cotangent,
    utt_bounds,
    live_blocks,
):
    rows = cotangent.shape[0]
    window = (2 * REACH + 1) * rows
    halo = lax.ppermute(features[-8:], "tm", [(i, i + 1) for i in range(size - 1)])
    flat_rows = subsample(
        features, halo, stem_kernel, mid_depthwise, mid_pointwise, last_depthwise, last_pointwise
    )
    cot_window = jnp.concatenate(gathered_window(cotangent, size), axis=0)
    d_attention = dot_nt(cot_window, out_weight).astype(jnp.bfloat16)

    my_index = lax.axis_index("tm")
    local_seg = segment_of(my_index * rows + jnp.arange(rows, dtype=jnp.int32), utt_bounds)
    window_seg = segment_of(
        (my_index - REACH) * rows + jnp.arange(window, dtype=jnp.int32), utt_bounds
    )
    flag = jnp.repeat(live_blocks[0], rows, total_repeat_length=window)
    bias = jnp.where(
        (window_seg[:, None] == local_seg[None, :]) & (flag[:, None] == 1), 0.0, neg_fill
    )
    bias2 = jnp.where(
        (local_seg[:, None] == window_seg[None, :]) & (flag[None, :] == 1), 0.0, neg_fill
    )

    frames = dot_nn(flat_rows, proj_weight).astype(jnp.bfloat16)
    frames_f = frames.astype(jnp.float32)
    row_mean = jnp.mean(frames_f, axis=-1, keepdims=True)
    centered = frames_f - row_mean
    inv_std = lax.rsqrt(jnp.mean(centered * centered, axis=-1, keepdims=True) + norm_eps)
    normalized = centered * inv_std
    normed = (normalized * norm_gain).astype(jnp.bfloat16)
    normed_window = jnp.concatenate(gathered_window(normed, size), axis=0)
    projected = dot_nn(normed_window, qkv_weight).astype(jnp.bfloat16)
    attention, stats = attention_forward(projected, d_attention, bias, rows)
    stats_window = jnp.stack(gathered_window(stats, size), axis=0)
    block_out = (frames_f + dot_nn(attention, out_weight)).astype(jnp.bfloat16)
    grads = attention_backward(projected, d_attention, stats_window, bias, bias2, rows)
    width = cotangent.shape[1]
    grad_normed = sum(
        dot_nt(g, qkv_weight[:, i * width : (i + 1) * width]) for i, g in enumerate(grads)
    )
    scaled_grad = grad_normed * norm_gain
    ln_grad = inv_std * (
        scaled_grad
        - jnp.mean(scaled_grad, axis=-1, keepdims=True)
        - normalized * jnp.mean(scaled_grad * normalized, axis=-1, keepdims=True)
    )
    frame_grads = (cotangent.astype(jnp.float32) + ln_grad).astype(jnp.bfloat16)
    own_cols = size * (flat_rows.shape[1] // size)
    columns = lax.all_to_all(flat_rows[:, :own_cols], "tm", 1, 0, tiled=True)
    all_grads = lax.all_gather(frame_grads, "tm", axis=0, tiled=True)
    proj_grads = dot_tn(columns, all_grads)
    return (block_out, frame_grads, proj_grads)


def solution(mesh):
    split = P(("groups", "tm"), None)
    in_specs = (split,) + (P(),) * 9 + (split, P("groups", None), split)
    return jax.shard_map(
        functools.partial(per_device, mesh.shape["tm"]),
        mesh=mesh,
        in_specs=in_specs,
        out_specs=(split, split, split),
        check_vma=False,
    )
```

```python
import functools

import jax
import jax.numpy as jnp
from jax import lax
from jax.experimental import pallas as pl
from jax.experimental.pallas import tpu as pltpu
from jax.sharding import PartitionSpec as P

HEADS = 8
REACH = 3
HEAD_DIM = 128
norm_eps = 1e-05
neg_fill = -1e30
MEL_PITCH = 84
SCALE = HEAD_DIM ** (-0.5)


def dot_nt(a, b):
    return lax.dot_general(a, b, (((1,), (1,)), ((), ())), preferred_element_type=jnp.float32)


def dot_tn(a, b):
    return lax.dot_general(a, b, (((0,), (0,)), ((), ())), preferred_element_type=jnp.float32)


def dot_nn(a, b):
    return jnp.dot(a, b, preferred_element_type=jnp.float32)


MESH = pl.DeviceIdType.MESH


class Exchange:
    def __init__(self, size, x_ref, out_ref, send, recv):
        self.size, self.x, self.out, self.send, self.recv = size, x_ref, out_ref, send, recv
        self.me = lax.axis_index("tm")
        self.odd = lax.rem(self.me, 2)
        self.sibling = self.me + 1 - 2 * self.odd
        self.far = self.me - 3 + 6 * self.odd
        self.has_low = self.me >= 2
        self.has_high = self.me + 2 < size
        self.has_far = jnp.logical_and(self.far >= 0, self.far < size)

    def copy(self, src, slot, sem, target):
        return pltpu.make_async_remote_copy(
            src_ref=src,
            dst_ref=self.out.at[slot],
            send_sem=self.send.at[sem],
            recv_sem=self.recv.at[sem],
            device_id={"tm": target},
            device_id_type=MESH,
        )

    def up(self):
        return self.copy(self.x, 1, 0, self.me + 2)

    def down(self):
        return self.copy(self.x, 5, 1, self.me - 2)

    def across(self):
        return self.copy(self.x, 2 + 2 * self.odd, 2, self.sibling)

    def remote(self):
        return self.copy(self.x, 6 - 6 * self.odd, 3, self.far)

    def pass_low(self):
        return self.copy(self.out.at[1], 2 * self.odd, 4, self.sibling)

    def pass_high(self):
        return self.copy(self.out.at[5], 4 + 2 * self.odd, 5, self.sibling)

    def local(self):
        return pltpu.make_async_copy(self.x, self.out.at[3], self.send.at[6])

    def begin(self):
        barrier = pltpu.get_barrier_semaphore()

        def greet(target):
            pl.semaphore_signal(barrier, inc=1, device_id={"tm": target}, device_id_type=MESH)

        greet(self.sibling)
        pl.when(self.has_low)(lambda: greet(self.me - 2))
        pl.when(self.has_high)(lambda: greet(self.me + 2))
        pl.when(self.has_far)(lambda: greet(self.far))
        self.local().start()
        for slot in range(7):
            if slot != 3:
                other = self.me + slot - 3
                outside = jnp.logical_or(other < 0, other >= self.size)

                @pl.when(outside)
                def _(slot=slot):
                    self.out[slot] = jnp.zeros(self.out.shape[1:], self.out.dtype)

        peers = 1
        for has in (self.has_low, self.has_high, self.has_far):
            peers += jnp.where(has, 1, 0)
        pl.semaphore_wait(barrier, peers)
        pl.when(self.has_high)(lambda: self.up().start())
        pl.when(self.has_low)(lambda: self.down().start())
        pl.when(self.has_far)(lambda: self.remote().start())
        self.across().start()

    def forward(self):
        @pl.when(self.has_low)
        def _():
            self.up().wait_recv()
            self.pass_low().start()

        @pl.when(self.has_high)
        def _():
            self.down().wait_recv()
            self.pass_high().start()

    def finish(self):
        self.local().wait()
        self.across().wait()
        pl.when(self.has_far)(lambda: self.remote().wait())

        @pl.when(self.has_low)
        def _():
            self.down().wait_send()
            self.pass_low().wait()

        @pl.when(self.has_high)
        def _():
            self.up().wait_send()
            self.pass_high().wait()


EXCHANGE_SEMS = [pltpu.SemaphoreType.DMA((7,)), pltpu.SemaphoreType.DMA((6,))]


def exchange_kernel(size, x_ref, out_ref, send, recv):
    exchange = Exchange(size, x_ref, out_ref, send, recv)
    exchange.begin()
    exchange.forward()
    exchange.finish()


def gathered_window(x, size):
    out = pl.pallas_call(
        functools.partial(exchange_kernel, size),
        out_shape=jax.ShapeDtypeStruct((7,) + x.shape, x.dtype),
        in_specs=[pl.BlockSpec(memory_space=pltpu.VMEM)],
        out_specs=pl.BlockSpec(memory_space=pltpu.VMEM),
        scratch_shapes=EXCHANGE_SEMS,
        compiler_params=pltpu.CompilerParams(collective_id=1, has_side_effects=True),
        name="exchange",
    )(x)
    return out.reshape((7 * x.shape[0],) + x.shape[1:])


def subsample_kernel(
    size,
    x_ref,
    stem_ref,
    mid_dw_ref,
    mid_pw_ref,
    last_dw_ref,
    last_pw_ref,
    cot_ref,
    flat_ref,
    window_ref,
    even,
    odd,
    second,
    shifted,
    send,
    recv,
):
    exchange = Exchange(size, cot_ref, window_ref, send, recv)
    exchange.begin()
    rows = x_ref.shape[0] // 4
    main = rows - 8
    mids = second.shape[0] - 1
    span = shifted.shape[1] - 256
    odd[0] = jnp.zeros(odd.shape[1:], odd.dtype)
    second[0] = jnp.zeros(second.shape[1:], second.dtype)
    for i in range(4):
        shifted[i] = stem_ref[8 - 2 * i : 8 - 2 * i + span + 256, :]

    def step(k, half):
        def stem(i):
            start = pl.multiple_of(span - 8 * k, 8)
            taps = shifted[i, pl.ds(start, 256), :].astype(jnp.bfloat16)
            return jnp.maximum(dot_nn(x_ref[...], taps), 0.0).reshape(even.shape)

        m = 2 * k + half
        even[...] = stem(2 * half)
        odd[1 - half] = stem(2 * half + 1)
        parts = (odd.at[half], even, odd.at[1 - half])
        early = jnp.zeros((main, 256), jnp.float32)
        late = jnp.zeros((rows, 256), jnp.float32)
        for df in range(3):
            src = parts[df]
            for dt in range(3):
                tap = mid_dw_ref[3 * dt + df : 3 * dt + df + 1, :]
                phase = (3, 0, 1)[dt]
                start = 7 if dt == 0 else 8
                early += src[phase, start : start + main, :] * tap
                late += src[dt + 1] * tap
        weight = mid_pw_ref[...]
        second[m + 1, 0, 8:rows, :] = jnp.maximum(dot_nn(early.astype(jnp.bfloat16), weight), 0.0)
        second[m + 1, 1] = jnp.maximum(dot_nn(late.astype(jnp.bfloat16), weight), 0.0)

    def body(k, _):
        step(k, 0)
        step(k, 1)
        return 0

    lax.fori_loop(0, mids // 2, body, 0)
    exchange.forward()
    for f in range(mids // 2):
        total = jnp.zeros((main, 256), jnp.float32)
        for df in range(3):
            for dt in range(3):
                tap = last_dw_ref[3 * dt + df : 3 * dt + df + 1, :]
                phase = (1, 0, 1)[dt]
                start = 7 if dt == 0 else 8
                total += second[2 * f + df, phase, start : start + main, :] * tap
        out = jnp.maximum(dot_nn(total.astype(jnp.bfloat16), last_pw_ref[...]), 0.0)
        flat_ref[:, f * 256 : (f + 1) * 256] = out.astype(jnp.bfloat16)
    exchange.finish()


def subsample(
    size,
    features,
    halo,
    stem_kernel,
    mid_depthwise,
    mid_pointwise,
    last_depthwise,
    last_pointwise,
    cotangent,
):
    feat_rows, mel = features.shape
    main = feat_rows // 8
    rows = main + 8
    channels = stem_kernel.shape[-1]
    mids = mel // 4
    series = jnp.concatenate([jnp.zeros((56, mel), features.dtype), halo, features], axis=0)
    series = jnp.pad(series, ((0, 0), (1, MEL_PITCH - mel - 1)))
    late = jnp.pad(series, ((1, 0), (0, 0)))[:-1].reshape(rows, 8 * MEL_PITCH)
    tail = series.reshape(rows, 8 * MEL_PITCH)[:, 7 * MEL_PITCH :]
    wide = jnp.concatenate([late, tail], axis=1)
    x = jnp.concatenate(
        [wide[:, 2 * p * MEL_PITCH : (2 * p + 3) * MEL_PITCH] for p in range(4)], axis=0
    )
    x = jnp.pad(x, ((0, 0), (0, 256 - 3 * MEL_PITCH)))
    base = jnp.pad(stem_kernel.astype(jnp.float32), ((0, 0), (0, MEL_PITCH - 3), (0, 0)))
    base = base.reshape(3 * MEL_PITCH, channels)
    base = jnp.pad(base, ((mel + 8, 256 - 3 * MEL_PITCH), (0, 0)))
    return pl.pallas_call(
        functools.partial(subsample_kernel, size),
        out_shape=(
            jax.ShapeDtypeStruct((main, (mids // 2) * channels), jnp.bfloat16),
            jax.ShapeDtypeStruct((7,) + cotangent.shape, jnp.bfloat16),
        ),
        in_specs=[pl.BlockSpec(memory_space=pltpu.VMEM)] * 7,
        out_specs=(pl.BlockSpec(memory_space=pltpu.VMEM),) * 2,
        scratch_shapes=[
            pltpu.VMEM((4, rows, channels), jnp.float32),
            pltpu.VMEM((2, 4, rows, channels), jnp.float32),
            pltpu.VMEM((mids + 1, 2, rows, channels), jnp.float32),
            pltpu.VMEM((4, mel + 256, channels), jnp.float32),
        ]
        + EXCHANGE_SEMS,
        compiler_params=pltpu.CompilerParams(
            vmem_limit_bytes=40 * 1024 * 1024, collective_id=0, has_side_effects=True
        ),
        cost_estimate=pl.CostEstimate(
            flops=20_000_000_000, bytes_accessed=2_000_000, transcendentals=0
        ),
        name="subsample",
    )(
        x,
        base,
        mid_depthwise.reshape(9, channels).astype(jnp.float32),
        mid_pointwise,
        last_depthwise.reshape(9, channels).astype(jnp.float32),
        last_pointwise,
        cotangent,
    )


def segments(positions, bounds_ref):
    found = jnp.zeros(positions.shape, jnp.int32)
    for u in range(bounds_ref.shape[0]):
        inside = (positions >= bounds_ref[u, 0]) & (positions < bounds_ref[u, 1])
        found = jnp.where(inside, u + 1, found)
    return found


def attention_kernel(
    size,
    proj_ref,
    do_ref,
    bounds_ref,
    live_ref,
    out_ref,
    grad_ref,
    bias_ref,
    bias2_ref,
    stat_ref,
    send,
    recv,
):
    rows = out_ref.shape[0]
    window = proj_ref.shape[0]
    width = out_ref.shape[1]
    own = slice(REACH * rows, (REACH + 1) * rows)
    me = lax.axis_index("tm")
    barrier = pltpu.get_barrier_semaphore()
    offsets = [o for o in range(-REACH, REACH + 1) if o]

    def when_there(offset, action):
        other = me + offset
        pl.when(jnp.logical_and(other >= 0, other < size))(lambda: action(offset))

    def greet(offset):
        pl.semaphore_signal(barrier, inc=1, device_id={"tm": me + offset}, device_id_type=MESH)

    def copy(offset):
        slot = REACH + offset
        return pltpu.make_async_remote_copy(
            src_ref=stat_ref.at[REACH],
            dst_ref=stat_ref.at[REACH - offset],
            send_sem=send.at[slot],
            recv_sem=recv.at[2 * REACH - slot],
            device_id={"tm": me + offset},
            device_id_type=MESH,
        )

    def incoming(offset):
        slot = REACH + offset
        return pltpu.make_async_remote_copy(
            src_ref=stat_ref.at[REACH],
            dst_ref=stat_ref.at[slot],
            send_sem=send.at[slot],
            recv_sem=recv.at[slot],
            device_id={"tm": me + offset},
            device_id_type=MESH,
        )

    for offset in offsets:
        when_there(offset, greet)

        @pl.when(jnp.logical_or(me + offset < 0, me + offset >= size))
        def _(offset=offset):
            stat_ref[REACH + offset] = jnp.zeros(stat_ref.shape[1:], jnp.float32)

    first = (me - REACH) * rows
    own_col = segments(me * rows + lax.broadcasted_iota(jnp.int32, (rows, 128), 0), bounds_ref)
    own_row = segments(me * rows + lax.broadcasted_iota(jnp.int32, (8, rows), 1), bounds_ref)[0:1]
    for b in range(2 * REACH + 1):
        place = first + b * rows
        live = live_ref[0, b] == 1
        col = segments(place + lax.broadcasted_iota(jnp.int32, (rows, 128), 0), bounds_ref)
        row = segments(place + lax.broadcasted_iota(jnp.int32, (8, rows), 1), bounds_ref)[0:1]
        span = slice(b * rows, (b + 1) * rows)
        bias_ref[span, :] = jnp.where((col[:, 0:1] == own_row) & live, 0.0, neg_fill)
        bias2_ref[:, span] = jnp.where((own_col[:, 0:1] == row) & live, 0.0, neg_fill)

    def column(group, h):
        return pl.ds(pl.multiple_of(group * width + h * HEAD_DIM, HEAD_DIM), HEAD_DIM)

    def forward(h):
        scores = dot_nt(proj_ref[:, column(1, h)], proj_ref[own, column(0, h)]) * SCALE
        scores = scores + bias_ref[...]
        top = jnp.max(scores, axis=0, keepdims=True)
        weights = jnp.exp(scores - top)
        total = jnp.sum(weights, axis=0, keepdims=True)
        probs = (weights * (1.0 / total)).astype(jnp.bfloat16)
        out = dot_tn(probs, proj_ref[:, column(2, h)])
        out_ref[:, column(0, h)] = out.astype(jnp.bfloat16)
        prod = do_ref[own, column(0, h)].astype(jnp.float32) * out
        stat_ref[REACH, h, 0:1, :] = top + jnp.log(total)
        stat_ref[REACH, h, 1:2, :] = jnp.sum(prod.T, axis=0, keepdims=True)

    def query_pass(h):
        keys = proj_ref[:, column(1, h)]
        scores = dot_nt(keys, proj_ref[own, column(0, h)]) * SCALE
        weights = jnp.exp(scores + bias_ref[...] - stat_ref[REACH, h, 0:1, :])
        dprob = dot_nt(proj_ref[:, column(2, h)], do_ref[own, column(0, h)])
        dscore = (weights * (dprob - stat_ref[REACH, h, 1:2, :])).astype(jnp.bfloat16)
        grad_ref[:, column(0, h)] = (dot_tn(dscore, keys) * SCALE).astype(jnp.bfloat16)

    def key_pass(h):
        queries = proj_ref[:, column(0, h)]
        douts = do_ref[:, column(0, h)]
        blocks = range(2 * REACH + 1)
        log_norms = jnp.concatenate([stat_ref[b, h, 0:1, :] for b in blocks], axis=1)
        deltas = jnp.concatenate([stat_ref[b, h, 1:2, :] for b in blocks], axis=1)
        scores = dot_nt(proj_ref[own, column(1, h)], queries) * SCALE
        weights = jnp.exp(scores + bias2_ref[...] - log_norms)
        dprob = dot_nt(proj_ref[own, column(2, h)], douts)
        dscore = (weights * (dprob - deltas)).astype(jnp.bfloat16)
        grad_ref[:, column(1, h)] = (dot_nn(dscore, queries) * SCALE).astype(jnp.bfloat16)
        grad_ref[:, column(2, h)] = dot_nn(weights.astype(jnp.bfloat16), douts).astype(jnp.bfloat16)

    def over_heads(work):
        def pair(i, _):
            work(2 * i)
            work(2 * i + 1)
            return 0

        lax.fori_loop(0, HEADS // 2, pair, 0)

    over_heads(forward)
    peers = 0
    for offset in offsets:
        peers += jnp.where(jnp.logical_and(me + offset >= 0, me + offset < size), 1, 0)
    pl.semaphore_wait(barrier, peers)
    for offset in offsets:
        when_there(offset, lambda o: copy(o).start())
    over_heads(query_pass)
    for offset in offsets:
        when_there(offset, lambda o: incoming(o).wait_recv())
    over_heads(key_pass)
    for offset in offsets:
        when_there(offset, lambda o: copy(o).wait_send())


def attention(size, projected, d_attention, utt_bounds, live_blocks):
    window = projected.shape[0]
    rows = window // (2 * REACH + 1)
    width = d_attention.shape[1]
    vmem = pl.BlockSpec(memory_space=pltpu.VMEM)
    smem = pl.BlockSpec(memory_space=pltpu.SMEM)
    return pl.pallas_call(
        functools.partial(attention_kernel, size),
        out_shape=(
            jax.ShapeDtypeStruct((rows, width), jnp.bfloat16),
            jax.ShapeDtypeStruct((rows, 3 * width), jnp.bfloat16),
        ),
        in_specs=[vmem, vmem, smem, smem],
        out_specs=(vmem, vmem),
        scratch_shapes=[
            pltpu.VMEM((window, rows), jnp.float32),
            pltpu.VMEM((rows, window), jnp.float32),
            pltpu.VMEM((2 * REACH + 1, HEADS, 2, rows), jnp.float32),
            pltpu.SemaphoreType.DMA((2 * REACH + 1,)),
            pltpu.SemaphoreType.DMA((2 * REACH + 1,)),
        ],
        compiler_params=pltpu.CompilerParams(
            vmem_limit_bytes=32 * 1024 * 1024, collective_id=2, has_side_effects=True
        ),
        cost_estimate=pl.CostEstimate(
            flops=20_000_000_000, bytes_accessed=8_000_000, transcendentals=2_000_000
        ),
        name="attention",
    )(projected, d_attention, utt_bounds, live_blocks)


def per_device(
    size,
    features,
    stem_kernel,
    mid_depthwise,
    mid_pointwise,
    last_depthwise,
    last_pointwise,
    proj_weight,
    norm_gain,
    qkv_weight,
    out_weight,
    cotangent,
    utt_bounds,
    live_blocks,
):
    halo = lax.ppermute(features[-8:], "tm", [(i, i + 1) for i in range(size - 1)])
    flat_rows, cot_window = subsample(
        size,
        features,
        halo,
        stem_kernel,
        mid_depthwise,
        mid_pointwise,
        last_depthwise,
        last_pointwise,
        cotangent,
    )
    cot_window = cot_window.reshape(-1, cotangent.shape[1])

    frames = dot_nn(flat_rows, proj_weight).astype(jnp.bfloat16)
    frames_f = frames.astype(jnp.float32)
    row_mean = jnp.mean(frames_f, axis=-1, keepdims=True)
    centered = frames_f - row_mean
    inv_std = lax.rsqrt(jnp.mean(centered * centered, axis=-1, keepdims=True) + norm_eps)
    normalized = centered * inv_std
    normed = (normalized * norm_gain).astype(jnp.bfloat16)
    normed_window = gathered_window(normed, size)
    normed_window, flat_sent, cot_window = lax.optimization_barrier(
        (normed_window, flat_rows, cot_window)
    )
    own_cols = size * (flat_rows.shape[1] // size)
    columns = lax.all_to_all(flat_sent[:, :own_cols], "tm", 1, 0, tiled=True)
    d_attention = dot_nt(cot_window, out_weight).astype(jnp.bfloat16)
    projected = dot_nn(normed_window, qkv_weight).astype(jnp.bfloat16)
    mixed, grads = attention(size, projected, d_attention, utt_bounds, live_blocks)
    grads, columns = lax.optimization_barrier((grads, columns))
    block_out = (frames_f + dot_nn(mixed, out_weight)).astype(jnp.bfloat16)
    grad_normed = dot_nt(grads, qkv_weight)
    scaled_grad = grad_normed * norm_gain
    ln_grad = inv_std * (
        scaled_grad
        - jnp.mean(scaled_grad, axis=-1, keepdims=True)
        - normalized * jnp.mean(scaled_grad * normalized, axis=-1, keepdims=True)
    )
    frame_grads = (cotangent.astype(jnp.float32) + ln_grad).astype(jnp.bfloat16)
    all_grads = lax.all_gather(frame_grads, "tm", axis=0, tiled=True)
    proj_grads = dot_tn(columns, all_grads)
    return (block_out, frame_grads, proj_grads)


def solution(mesh):
    split = P(("groups", "tm"), None)
    in_specs = (split,) + (P(),) * 9 + (split, P("groups", None), split)
    return jax.shard_map(
        functools.partial(per_device, mesh.shape["tm"]),
        mesh=mesh,
        in_specs=in_specs,
        out_specs=(split, split, split),
        check_vma=False,
    )
```

```python
import functools

import jax
import jax.numpy as jnp
from jax import lax
from jax.experimental import pallas as pl
from jax.experimental.pallas import tpu as pltpu
from jax.sharding import PartitionSpec as P

HEADS = 8
REACH = 3
HEAD_DIM = 128
norm_eps = 1e-05
neg_fill = -1e30
MEL_PITCH = 84
SCALE = HEAD_DIM ** (-0.5)


def dot_nt(a, b):
    return lax.dot_general(a, b, (((1,), (1,)), ((), ())), preferred_element_type=jnp.float32)


def dot_tn(a, b):
    return lax.dot_general(a, b, (((0,), (0,)), ((), ())), preferred_element_type=jnp.float32)


def dot_nn(a, b):
    return jnp.dot(a, b, preferred_element_type=jnp.float32)


MESH = pl.DeviceIdType.MESH


class Exchange:
    def __init__(self, size, x_ref, out_ref, send, recv):
        self.size, self.x, self.out, self.send, self.recv = size, x_ref, out_ref, send, recv
        self.me = lax.axis_index("tm")
        self.odd = lax.rem(self.me, 2)
        self.sibling = self.me + 1 - 2 * self.odd
        self.far = self.me - 3 + 6 * self.odd
        self.has_low = self.me >= 2
        self.has_high = self.me + 2 < size
        self.has_far = jnp.logical_and(self.far >= 0, self.far < size)

    def copy(self, src, slot, sem, target):
        return pltpu.make_async_remote_copy(
            src_ref=src,
            dst_ref=self.out.at[slot],
            send_sem=self.send.at[sem],
            recv_sem=self.recv.at[sem],
            device_id={"tm": target},
            device_id_type=MESH,
        )

    def up(self):
        return self.copy(self.x, 1, 0, self.me + 2)

    def down(self):
        return self.copy(self.x, 5, 1, self.me - 2)

    def across(self):
        return self.copy(self.x, 2 + 2 * self.odd, 2, self.sibling)

    def remote(self):
        return self.copy(self.x, 6 - 6 * self.odd, 3, self.far)

    def pass_low(self):
        return self.copy(self.out.at[1], 2 * self.odd, 4, self.sibling)

    def pass_high(self):
        return self.copy(self.out.at[5], 4 + 2 * self.odd, 5, self.sibling)

    def local(self):
        return pltpu.make_async_copy(self.x, self.out.at[3], self.send.at[6])

    def begin(self):
        barrier = pltpu.get_barrier_semaphore()

        def greet(target):
            pl.semaphore_signal(barrier, inc=1, device_id={"tm": target}, device_id_type=MESH)

        greet(self.sibling)
        pl.when(self.has_low)(lambda: greet(self.me - 2))
        pl.when(self.has_high)(lambda: greet(self.me + 2))
        pl.when(self.has_far)(lambda: greet(self.far))
        self.local().start()
        for slot in range(7):
            if slot != 3:
                other = self.me + slot - 3
                outside = jnp.logical_or(other < 0, other >= self.size)

                @pl.when(outside)
                def _(slot=slot):
                    self.out[slot] = jnp.zeros(self.out.shape[1:], self.out.dtype)

        peers = 1
        for has in (self.has_low, self.has_high, self.has_far):
            peers += jnp.where(has, 1, 0)
        pl.semaphore_wait(barrier, peers)
        pl.when(self.has_high)(lambda: self.up().start())
        pl.when(self.has_low)(lambda: self.down().start())
        pl.when(self.has_far)(lambda: self.remote().start())
        self.across().start()

    def forward(self):
        @pl.when(self.has_low)
        def _():
            self.up().wait_recv()
            self.pass_low().start()

        @pl.when(self.has_high)
        def _():
            self.down().wait_recv()
            self.pass_high().start()

    def finish(self):
        self.local().wait()
        self.across().wait()
        pl.when(self.has_far)(lambda: self.remote().wait())

        @pl.when(self.has_low)
        def _():
            self.down().wait_send()
            self.pass_low().wait()

        @pl.when(self.has_high)
        def _():
            self.up().wait_send()
            self.pass_high().wait()


EXCHANGE_SEMS = [pltpu.SemaphoreType.DMA((7,)), pltpu.SemaphoreType.DMA((6,))]


def exchange_kernel(size, x_ref, out_ref, send, recv):
    exchange = Exchange(size, x_ref, out_ref, send, recv)
    exchange.begin()
    exchange.forward()
    exchange.finish()


def gathered_window(x, size):
    out = pl.pallas_call(
        functools.partial(exchange_kernel, size),
        out_shape=jax.ShapeDtypeStruct((7,) + x.shape, x.dtype),
        in_specs=[pl.BlockSpec(memory_space=pltpu.VMEM)],
        out_specs=pl.BlockSpec(memory_space=pltpu.VMEM),
        scratch_shapes=EXCHANGE_SEMS,
        compiler_params=pltpu.CompilerParams(collective_id=1, has_side_effects=True),
        name="exchange",
    )(x)
    return out.reshape((7 * x.shape[0],) + x.shape[1:])


def gather_kernel(size, x_ref, out_ref, send, recv, side_send, side_recv, own_sem):
    chips = size // 2
    half = chips // 2
    rows = x_ref.shape[0]
    piece = rows // 2
    me = lax.axis_index("tm")
    core = lax.rem(me, 2)
    chip = me // 2
    sibling = me + 1 - 2 * core
    odd = lax.rem(chip, 2)
    place = jnp.where(odd == 0, chip // 2, chips - 1 - chip // 2)

    def device(offset):
        spot = lax.rem(place + offset + 2 * chips, chips)
        return jnp.where(spot < half, 2 * spot, 2 * (chips - 1 - spot) + 1) * 2 + core

    def remote(src, dst, send_sem, recv_sem, target):
        return pltpu.make_async_remote_copy(
            src_ref=src,
            dst_ref=dst,
            send_sem=send_sem,
            recv_sem=recv_sem,
            device_id={"tm": target},
            device_id_type=MESH,
        )

    def part(slot, c):
        return out_ref.at[slot, pl.ds(c * piece, piece), :]

    def along(way, k, c):
        sign = 1 - 2 * way
        slot = device(-sign * (k - 1))
        src = x_ref.at[pl.ds(c * piece, piece), :] if k == 1 else part(slot, c)
        index = (way, k - 1, c)
        return remote(src, part(slot, c), send.at[index], recv.at[index], device(sign))

    def arrived(way, k, c):
        sign = 1 - 2 * way
        slot = device(-sign * k)
        index = (way, k - 1, c)
        return remote(part(slot, c), part(slot, c), send.at[index], recv.at[index], device(sign))

    def side(way, k, c):
        slot = device(-(1 - 2 * way) * k)
        index = (way, k - 1, c)
        return remote(part(slot, c), part(slot, c), side_send.at[index], side_recv.at[index], sibling)

    def side_arrived(way, k, c):
        slot = device(-(1 - 2 * way) * k) + 1 - 2 * core
        index = (way, k - 1, c)
        return remote(part(slot, c), part(slot, c), side_send.at[index], side_recv.at[index], sibling)

    def used(way, k, c):
        return k < half or (k == half and c == way)

    steps = [
        (way, k, c)
        for k in range(1, half + 1)
        for c in range(2)
        for way in range(2)
        if used(way, k, c)
    ]
    barrier = pltpu.get_barrier_semaphore()
    for target in (device(1), device(-1), sibling):
        pl.semaphore_signal(barrier, inc=1, device_id={"tm": target}, device_id_type=MESH)
    own = pltpu.make_async_copy(x_ref, out_ref.at[me], own_sem.at[0])
    across = remote(x_ref, out_ref.at[me], own_sem.at[1], own_sem.at[2], sibling)
    own.start()
    pl.semaphore_wait(barrier, 3)
    for c in range(2):
        for way in range(2):
            along(way, 1, c).start()
    across.start()
    for way, k, c in steps:
        arrived(way, k, c).wait_recv()
        if used(way, k + 1, c):
            along(way, k + 1, c).start()
        side(way, k, c).start()
    own.wait()
    across.wait()
    for way, k, c in steps:
        side_arrived(way, k, c).wait_recv()
        side(way, k, c).wait_send()
        along(way, k, c).wait_send()


def gathered(x, size):
    half = size // 4
    out = pl.pallas_call(
        functools.partial(gather_kernel, size),
        out_shape=jax.ShapeDtypeStruct((size,) + x.shape, x.dtype),
        in_specs=[pl.BlockSpec(memory_space=pltpu.VMEM)],
        out_specs=pl.BlockSpec(memory_space=pltpu.VMEM),
        scratch_shapes=[pltpu.SemaphoreType.DMA((2, half, 2))] * 4
        + [pltpu.SemaphoreType.DMA((3,))],
        compiler_params=pltpu.CompilerParams(
            vmem_limit_bytes=32 * 1024 * 1024, collective_id=3, has_side_effects=True
        ),
        name="all_gather",
    )(x)
    return out.reshape((size * x.shape[0],) + x.shape[1:])


def subsample_kernel(
    size,
    x_ref,
    stem_ref,
    mid_dw_ref,
    mid_pw_ref,
    last_dw_ref,
    last_pw_ref,
    cot_ref,
    flat_ref,
    window_ref,
    even,
    odd,
    second,
    shifted,
    send,
    recv,
):
    exchange = Exchange(size, cot_ref, window_ref, send, recv)
    exchange.begin()
    rows = x_ref.shape[0] // 4
    main = rows - 8
    mids = second.shape[0] - 1
    span = shifted.shape[1] - 256
    odd[0] = jnp.zeros(odd.shape[1:], odd.dtype)
    second[0] = jnp.zeros(second.shape[1:], second.dtype)
    for i in range(4):
        shifted[i] = stem_ref[8 - 2 * i : 8 - 2 * i + span + 256, :]

    def step(k, half):
        def stem(i):
            start = pl.multiple_of(span - 8 * k, 8)
            taps = shifted[i, pl.ds(start, 256), :].astype(jnp.bfloat16)
            return jnp.maximum(dot_nn(x_ref[...], taps), 0.0).reshape(even.shape)

        m = 2 * k + half
        even[...] = stem(2 * half)
        odd[1 - half] = stem(2 * half + 1)
        parts = (odd.at[half], even, odd.at[1 - half])
        early = jnp.zeros((main, 256), jnp.float32)
        late = jnp.zeros((rows, 256), jnp.float32)
        for df in range(3):
            src = parts[df]
            for dt in range(3):
                tap = mid_dw_ref[3 * dt + df : 3 * dt + df + 1, :]
                phase = (3, 0, 1)[dt]
                start = 7 if dt == 0 else 8
                early += src[phase, start : start + main, :] * tap
                late += src[dt + 1] * tap
        weight = mid_pw_ref[...]
        second[m + 1, 0, 8:rows, :] = jnp.maximum(dot_nn(early.astype(jnp.bfloat16), weight), 0.0)
        second[m + 1, 1] = jnp.maximum(dot_nn(late.astype(jnp.bfloat16), weight), 0.0)

    def body(k, _):
        step(k, 0)
        step(k, 1)
        return 0

    lax.fori_loop(0, mids // 2, body, 0)
    exchange.forward()
    for f in range(mids // 2):
        total = jnp.zeros((main, 256), jnp.float32)
        for df in range(3):
            for dt in range(3):
                tap = last_dw_ref[3 * dt + df : 3 * dt + df + 1, :]
                phase = (1, 0, 1)[dt]
                start = 7 if dt == 0 else 8
                total += second[2 * f + df, phase, start : start + main, :] * tap
        out = jnp.maximum(dot_nn(total.astype(jnp.bfloat16), last_pw_ref[...]), 0.0)
        flat_ref[:, f * 256 : (f + 1) * 256] = out.astype(jnp.bfloat16)
    exchange.finish()


def subsample(
    size,
    features,
    halo,
    stem_kernel,
    mid_depthwise,
    mid_pointwise,
    last_depthwise,
    last_pointwise,
    cotangent,
):
    feat_rows, mel = features.shape
    main = feat_rows // 8
    rows = main + 8
    channels = stem_kernel.shape[-1]
    mids = mel // 4
    series = jnp.concatenate([jnp.zeros((56, mel), features.dtype), halo, features], axis=0)
    series = jnp.pad(series, ((0, 0), (1, MEL_PITCH - mel - 1)))
    late = jnp.pad(series, ((1, 0), (0, 0)))[:-1].reshape(rows, 8 * MEL_PITCH)
    tail = series.reshape(rows, 8 * MEL_PITCH)[:, 7 * MEL_PITCH :]
    wide = jnp.concatenate([late, tail], axis=1)
    x = jnp.concatenate(
        [wide[:, 2 * p * MEL_PITCH : (2 * p + 3) * MEL_PITCH] for p in range(4)], axis=0
    )
    x = jnp.pad(x, ((0, 0), (0, 256 - 3 * MEL_PITCH)))
    base = jnp.pad(stem_kernel.astype(jnp.float32), ((0, 0), (0, MEL_PITCH - 3), (0, 0)))
    base = base.reshape(3 * MEL_PITCH, channels)
    base = jnp.pad(base, ((mel + 8, 256 - 3 * MEL_PITCH), (0, 0)))
    return pl.pallas_call(
        functools.partial(subsample_kernel, size),
        out_shape=(
            jax.ShapeDtypeStruct((main, (mids // 2) * channels), jnp.bfloat16),
            jax.ShapeDtypeStruct((7,) + cotangent.shape, jnp.bfloat16),
        ),
        in_specs=[pl.BlockSpec(memory_space=pltpu.VMEM)] * 7,
        out_specs=(pl.BlockSpec(memory_space=pltpu.VMEM),) * 2,
        scratch_shapes=[
            pltpu.VMEM((4, rows, channels), jnp.float32),
            pltpu.VMEM((2, 4, rows, channels), jnp.float32),
            pltpu.VMEM((mids + 1, 2, rows, channels), jnp.float32),
            pltpu.VMEM((4, mel + 256, channels), jnp.float32),
        ]
        + EXCHANGE_SEMS,
        compiler_params=pltpu.CompilerParams(
            vmem_limit_bytes=40 * 1024 * 1024, collective_id=0, has_side_effects=True
        ),
        cost_estimate=pl.CostEstimate(
            flops=20_000_000_000, bytes_accessed=2_000_000, transcendentals=0
        ),
        name="subsample",
    )(
        x,
        base,
        mid_depthwise.reshape(9, channels).astype(jnp.float32),
        mid_pointwise,
        last_depthwise.reshape(9, channels).astype(jnp.float32),
        last_pointwise,
        cotangent,
    )


def segments(positions, bounds_ref):
    found = jnp.zeros(positions.shape, jnp.int32)
    for u in range(bounds_ref.shape[0]):
        inside = (positions >= bounds_ref[u, 0]) & (positions < bounds_ref[u, 1])
        found = jnp.where(inside, u + 1, found)
    return found


def attention_kernel(
    size,
    proj_ref,
    do_ref,
    bounds_ref,
    live_ref,
    out_ref,
    grad_ref,
    bias_ref,
    bias2_ref,
    stat_ref,
    send,
    recv,
):
    rows = out_ref.shape[0]
    window = proj_ref.shape[0]
    width = out_ref.shape[1]
    own = slice(REACH * rows, (REACH + 1) * rows)
    me = lax.axis_index("tm")
    barrier = pltpu.get_barrier_semaphore()
    offsets = [o for o in range(-REACH, REACH + 1) if o]

    def when_there(offset, action):
        other = me + offset
        pl.when(jnp.logical_and(other >= 0, other < size))(lambda: action(offset))

    def greet(offset):
        pl.semaphore_signal(barrier, inc=1, device_id={"tm": me + offset}, device_id_type=MESH)

    def copy(offset):
        slot = REACH + offset
        return pltpu.make_async_remote_copy(
            src_ref=stat_ref.at[REACH],
            dst_ref=stat_ref.at[REACH - offset],
            send_sem=send.at[slot],
            recv_sem=recv.at[2 * REACH - slot],
            device_id={"tm": me + offset},
            device_id_type=MESH,
        )

    def incoming(offset):
        slot = REACH + offset
        return pltpu.make_async_remote_copy(
            src_ref=stat_ref.at[REACH],
            dst_ref=stat_ref.at[slot],
            send_sem=send.at[slot],
            recv_sem=recv.at[slot],
            device_id={"tm": me + offset},
            device_id_type=MESH,
        )

    for offset in offsets:
        when_there(offset, greet)

        @pl.when(jnp.logical_or(me + offset < 0, me + offset >= size))
        def _(offset=offset):
            stat_ref[REACH + offset] = jnp.zeros(stat_ref.shape[1:], jnp.float32)

    first = (me - REACH) * rows
    own_col = segments(me * rows + lax.broadcasted_iota(jnp.int32, (rows, 128), 0), bounds_ref)
    own_row = segments(me * rows + lax.broadcasted_iota(jnp.int32, (8, rows), 1), bounds_ref)[0:1]
    for b in range(2 * REACH + 1):
        place = first + b * rows
        live = live_ref[0, b] == 1
        col = segments(place + lax.broadcasted_iota(jnp.int32, (rows, 128), 0), bounds_ref)
        row = segments(place + lax.broadcasted_iota(jnp.int32, (8, rows), 1), bounds_ref)[0:1]
        span = slice(b * rows, (b + 1) * rows)
        bias_ref[span, :] = jnp.where((col[:, 0:1] == own_row) & live, 0.0, neg_fill)
        bias2_ref[:, span] = jnp.where((own_col[:, 0:1] == row) & live, 0.0, neg_fill)

    def column(group, h):
        return pl.ds(pl.multiple_of(group * width + h * HEAD_DIM, HEAD_DIM), HEAD_DIM)

    def forward(h):
        scores = dot_nt(proj_ref[:, column(1, h)], proj_ref[own, column(0, h)]) * SCALE
        scores = scores + bias_ref[...]
        top = jnp.max(scores, axis=0, keepdims=True)
        weights = jnp.exp(scores - top)
        total = jnp.sum(weights, axis=0, keepdims=True)
        probs = (weights * (1.0 / total)).astype(jnp.bfloat16)
        out = dot_tn(probs, proj_ref[:, column(2, h)])
        out_ref[:, column(0, h)] = out.astype(jnp.bfloat16)
        prod = do_ref[own, column(0, h)].astype(jnp.float32) * out
        stat_ref[REACH, h, 0:1, :] = top + jnp.log(total)
        stat_ref[REACH, h, 1:2, :] = jnp.sum(prod.T, axis=0, keepdims=True)

    def query_pass(h):
        keys = proj_ref[:, column(1, h)]
        scores = dot_nt(keys, proj_ref[own, column(0, h)]) * SCALE
        weights = jnp.exp(scores + bias_ref[...] - stat_ref[REACH, h, 0:1, :])
        dprob = dot_nt(proj_ref[:, column(2, h)], do_ref[own, column(0, h)])
        dscore = (weights * (dprob - stat_ref[REACH, h, 1:2, :])).astype(jnp.bfloat16)
        grad_ref[:, column(0, h)] = (dot_tn(dscore, keys) * SCALE).astype(jnp.bfloat16)

    def key_pass(h):
        queries = proj_ref[:, column(0, h)]
        douts = do_ref[:, column(0, h)]
        blocks = range(2 * REACH + 1)
        log_norms = jnp.concatenate([stat_ref[b, h, 0:1, :] for b in blocks], axis=1)
        deltas = jnp.concatenate([stat_ref[b, h, 1:2, :] for b in blocks], axis=1)
        scores = dot_nt(proj_ref[own, column(1, h)], queries) * SCALE
        weights = jnp.exp(scores + bias2_ref[...] - log_norms)
        dprob = dot_nt(proj_ref[own, column(2, h)], douts)
        dscore = (weights * (dprob - deltas)).astype(jnp.bfloat16)
        grad_ref[:, column(1, h)] = (dot_nn(dscore, queries) * SCALE).astype(jnp.bfloat16)
        grad_ref[:, column(2, h)] = dot_nn(weights.astype(jnp.bfloat16), douts).astype(jnp.bfloat16)

    def over_heads(work):
        def pair(i, _):
            work(2 * i)
            work(2 * i + 1)
            return 0

        lax.fori_loop(0, HEADS // 2, pair, 0)

    over_heads(forward)
    peers = 0
    for offset in offsets:
        peers += jnp.where(jnp.logical_and(me + offset >= 0, me + offset < size), 1, 0)
    pl.semaphore_wait(barrier, peers)
    for offset in offsets:
        when_there(offset, lambda o: copy(o).start())
    over_heads(query_pass)
    for offset in offsets:
        when_there(offset, lambda o: incoming(o).wait_recv())
    over_heads(key_pass)
    for offset in offsets:
        when_there(offset, lambda o: copy(o).wait_send())


def attention(size, projected, d_attention, utt_bounds, live_blocks):
    window = projected.shape[0]
    rows = window // (2 * REACH + 1)
    width = d_attention.shape[1]
    vmem = pl.BlockSpec(memory_space=pltpu.VMEM)
    smem = pl.BlockSpec(memory_space=pltpu.SMEM)
    return pl.pallas_call(
        functools.partial(attention_kernel, size),
        out_shape=(
            jax.ShapeDtypeStruct((rows, width), jnp.bfloat16),
            jax.ShapeDtypeStruct((rows, 3 * width), jnp.bfloat16),
        ),
        in_specs=[vmem, vmem, smem, smem],
        out_specs=(vmem, vmem),
        scratch_shapes=[
            pltpu.VMEM((window, rows), jnp.float32),
            pltpu.VMEM((rows, window), jnp.float32),
            pltpu.VMEM((2 * REACH + 1, HEADS, 2, rows), jnp.float32),
            pltpu.SemaphoreType.DMA((2 * REACH + 1,)),
            pltpu.SemaphoreType.DMA((2 * REACH + 1,)),
        ],
        compiler_params=pltpu.CompilerParams(
            vmem_limit_bytes=32 * 1024 * 1024, collective_id=2, has_side_effects=True
        ),
        cost_estimate=pl.CostEstimate(
            flops=20_000_000_000, bytes_accessed=8_000_000, transcendentals=2_000_000
        ),
        name="attention",
    )(projected, d_attention, utt_bounds, live_blocks)


def per_device(
    size,
    features,
    stem_kernel,
    mid_depthwise,
    mid_pointwise,
    last_depthwise,
    last_pointwise,
    proj_weight,
    norm_gain,
    qkv_weight,
    out_weight,
    cotangent,
    utt_bounds,
    live_blocks,
):
    halo = lax.ppermute(features[-8:], "tm", [(i, i + 1) for i in range(size - 1)])
    flat_rows, cot_window = subsample(
        size,
        features,
        halo,
        stem_kernel,
        mid_depthwise,
        mid_pointwise,
        last_depthwise,
        last_pointwise,
        cotangent,
    )
    cot_window = cot_window.reshape(-1, cotangent.shape[1])

    frames = dot_nn(flat_rows, proj_weight).astype(jnp.bfloat16)
    frames_f = frames.astype(jnp.float32)
    row_mean = jnp.mean(frames_f, axis=-1, keepdims=True)
    centered = frames_f - row_mean
    inv_std = lax.rsqrt(jnp.mean(centered * centered, axis=-1, keepdims=True) + norm_eps)
    normalized = centered * inv_std
    normed = (normalized * norm_gain).astype(jnp.bfloat16)
    normed_window = gathered_window(normed, size)
    normed_window, flat_sent, cot_window = lax.optimization_barrier(
        (normed_window, flat_rows, cot_window)
    )
    own_cols = size * (flat_rows.shape[1] // size)
    columns = lax.all_to_all(flat_sent[:, :own_cols], "tm", 1, 0, tiled=True)
    d_attention = dot_nt(cot_window, out_weight).astype(jnp.bfloat16)
    projected = dot_nn(normed_window, qkv_weight).astype(jnp.bfloat16)
    mixed, grads = attention(size, projected, d_attention, utt_bounds, live_blocks)
    grads, columns = lax.optimization_barrier((grads, columns))
    block_out = (frames_f + dot_nn(mixed, out_weight)).astype(jnp.bfloat16)
    grad_normed = dot_nt(grads, qkv_weight)
    scaled_grad = grad_normed * norm_gain
    ln_grad = inv_std * (
        scaled_grad
        - jnp.mean(scaled_grad, axis=-1, keepdims=True)
        - normalized * jnp.mean(scaled_grad * normalized, axis=-1, keepdims=True)
    )
    frame_grads = (cotangent.astype(jnp.float32) + ln_grad).astype(jnp.bfloat16)
    all_grads = gathered(frame_grads, size)
    proj_grads = dot_tn(columns, all_grads)
    return (block_out, frame_grads, proj_grads)


def solution(mesh):
    split = P(("groups", "tm"), None)
    in_specs = (split,) + (P(),) * 9 + (split, P("groups", None), split)
    return jax.shard_map(
        functools.partial(per_device, mesh.shape["tm"]),
        mesh=mesh,
        in_specs=in_specs,
        out_specs=(split, split, split),
        check_vma=False,
    )
```

```python
import functools

import jax
import jax.numpy as jnp
from jax import lax
from jax.experimental import pallas as pl
from jax.experimental.pallas import tpu as pltpu
from jax.sharding import PartitionSpec as P

HEADS = 8
REACH = 3
HEAD_DIM = 128
norm_eps = 1e-05
neg_fill = -1e30
MEL_PITCH = 84
SCALE = HEAD_DIM ** (-0.5)


def dot_nt(a, b):
    return lax.dot_general(a, b, (((1,), (1,)), ((), ())), preferred_element_type=jnp.float32)


def dot_tn(a, b):
    return lax.dot_general(a, b, (((0,), (0,)), ((), ())), preferred_element_type=jnp.float32)


def dot_nn(a, b):
    return jnp.dot(a, b, preferred_element_type=jnp.float32)


MESH = pl.DeviceIdType.MESH


class Exchange:
    def __init__(self, size, x_ref, out_ref, send, recv):
        self.size, self.x, self.out, self.send, self.recv = size, x_ref, out_ref, send, recv
        self.me = lax.axis_index("tm")
        self.odd = lax.rem(self.me, 2)
        self.sibling = self.me + 1 - 2 * self.odd
        self.far = self.me - 3 + 6 * self.odd
        self.has_low = self.me >= 2
        self.has_high = self.me + 2 < size
        self.has_far = jnp.logical_and(self.far >= 0, self.far < size)

    def copy(self, src, slot, sem, target):
        return pltpu.make_async_remote_copy(
            src_ref=src,
            dst_ref=self.out.at[slot],
            send_sem=self.send.at[sem],
            recv_sem=self.recv.at[sem],
            device_id={"tm": target},
            device_id_type=MESH,
        )

    def up(self):
        return self.copy(self.x, 1, 0, self.me + 2)

    def down(self):
        return self.copy(self.x, 5, 1, self.me - 2)

    def across(self):
        return self.copy(self.x, 2 + 2 * self.odd, 2, self.sibling)

    def remote(self):
        return self.copy(self.x, 6 - 6 * self.odd, 3, self.far)

    def pass_low(self):
        return self.copy(self.out.at[1], 2 * self.odd, 4, self.sibling)

    def pass_high(self):
        return self.copy(self.out.at[5], 4 + 2 * self.odd, 5, self.sibling)

    def local(self):
        return pltpu.make_async_copy(self.x, self.out.at[3], self.send.at[6])

    def begin(self):
        barrier = pltpu.get_barrier_semaphore()

        def greet(target):
            pl.semaphore_signal(barrier, inc=1, device_id={"tm": target}, device_id_type=MESH)

        greet(self.sibling)
        pl.when(self.has_low)(lambda: greet(self.me - 2))
        pl.when(self.has_high)(lambda: greet(self.me + 2))
        pl.when(self.has_far)(lambda: greet(self.far))
        self.local().start()
        for slot in range(7):
            if slot != 3:
                other = self.me + slot - 3
                outside = jnp.logical_or(other < 0, other >= self.size)

                @pl.when(outside)
                def _(slot=slot):
                    self.out[slot] = jnp.zeros(self.out.shape[1:], self.out.dtype)

        peers = 1
        for has in (self.has_low, self.has_high, self.has_far):
            peers += jnp.where(has, 1, 0)
        pl.semaphore_wait(barrier, peers)
        pl.when(self.has_high)(lambda: self.up().start())
        pl.when(self.has_low)(lambda: self.down().start())
        pl.when(self.has_far)(lambda: self.remote().start())
        self.across().start()

    def forward(self):
        @pl.when(self.has_low)
        def _():
            self.up().wait_recv()
            self.pass_low().start()

        @pl.when(self.has_high)
        def _():
            self.down().wait_recv()
            self.pass_high().start()

    def finish(self):
        self.local().wait()
        self.across().wait()
        pl.when(self.has_far)(lambda: self.remote().wait())

        @pl.when(self.has_low)
        def _():
            self.down().wait_send()
            self.pass_low().wait()

        @pl.when(self.has_high)
        def _():
            self.up().wait_send()
            self.pass_high().wait()


EXCHANGE_SEMS = [pltpu.SemaphoreType.DMA((7,)), pltpu.SemaphoreType.DMA((6,))]


def exchange_kernel(size, x_ref, out_ref, send, recv):
    exchange = Exchange(size, x_ref, out_ref, send, recv)
    exchange.begin()
    exchange.forward()
    exchange.finish()


def gathered_window(x, size):
    out = pl.pallas_call(
        functools.partial(exchange_kernel, size),
        out_shape=jax.ShapeDtypeStruct((7,) + x.shape, x.dtype),
        in_specs=[pl.BlockSpec(memory_space=pltpu.VMEM)],
        out_specs=pl.BlockSpec(memory_space=pltpu.VMEM),
        scratch_shapes=EXCHANGE_SEMS,
        compiler_params=pltpu.CompilerParams(collective_id=1, has_side_effects=True),
        name="exchange",
    )(x)
    return out.reshape((7 * x.shape[0],) + x.shape[1:])


def gather_kernel(size, x_ref, out_ref, send, recv, side_send, side_recv, own_sem):
    chips = size // 2
    half = chips // 2
    rows = x_ref.shape[0]
    piece = rows // 2
    me = lax.axis_index("tm")
    core = lax.rem(me, 2)
    chip = me // 2
    sibling = me + 1 - 2 * core
    odd = lax.rem(chip, 2)
    place = jnp.where(odd == 0, chip // 2, chips - 1 - chip // 2)

    def device(offset):
        spot = lax.rem(place + offset + 2 * chips, chips)
        return jnp.where(spot < half, 2 * spot, 2 * (chips - 1 - spot) + 1) * 2 + core

    def remote(src, dst, send_sem, recv_sem, target):
        return pltpu.make_async_remote_copy(
            src_ref=src,
            dst_ref=dst,
            send_sem=send_sem,
            recv_sem=recv_sem,
            device_id={"tm": target},
            device_id_type=MESH,
        )

    def part(slot, c):
        return out_ref.at[slot, pl.ds(c * piece, piece), :]

    def along(way, k, c):
        sign = 1 - 2 * way
        slot = device(-sign * (k - 1))
        src = x_ref.at[pl.ds(c * piece, piece), :] if k == 1 else part(slot, c)
        index = (way, k - 1, c)
        return remote(src, part(slot, c), send.at[index], recv.at[index], device(sign))

    def arrived(way, k, c):
        sign = 1 - 2 * way
        slot = device(-sign * k)
        index = (way, k - 1, c)
        return remote(part(slot, c), part(slot, c), send.at[index], recv.at[index], device(sign))

    def side(way, k, c):
        slot = device(-(1 - 2 * way) * k)
        index = (way, k - 1, c)
        return remote(part(slot, c), part(slot, c), side_send.at[index], side_recv.at[index], sibling)

    def side_arrived(way, k, c):
        slot = device(-(1 - 2 * way) * k) + 1 - 2 * core
        index = (way, k - 1, c)
        return remote(part(slot, c), part(slot, c), side_send.at[index], side_recv.at[index], sibling)

    def used(way, k, c):
        return k < half or (k == half and c == way)

    steps = [
        (way, k, c)
        for k in range(1, half + 1)
        for c in range(2)
        for way in range(2)
        if used(way, k, c)
    ]
    barrier = pltpu.get_barrier_semaphore()
    for target in (device(1), device(-1), sibling):
        pl.semaphore_signal(barrier, inc=1, device_id={"tm": target}, device_id_type=MESH)
    own = pltpu.make_async_copy(x_ref, out_ref.at[me], own_sem.at[0])
    across = remote(x_ref, out_ref.at[me], own_sem.at[1], own_sem.at[2], sibling)
    own.start()
    pl.semaphore_wait(barrier, 3)
    for c in range(2):
        for way in range(2):
            along(way, 1, c).start()
    across.start()
    for way, k, c in steps:
        arrived(way, k, c).wait_recv()
        if used(way, k + 1, c):
            along(way, k + 1, c).start()
        side(way, k, c).start()
    own.wait()
    across.wait()
    for way, k, c in steps:
        side_arrived(way, k, c).wait_recv()
        side(way, k, c).wait_send()
        along(way, k, c).wait_send()


def gathered(x, size):
    half = size // 4
    out = pl.pallas_call(
        functools.partial(gather_kernel, size),
        out_shape=jax.ShapeDtypeStruct((size,) + x.shape, x.dtype),
        in_specs=[pl.BlockSpec(memory_space=pltpu.VMEM)],
        out_specs=pl.BlockSpec(memory_space=pltpu.VMEM),
        scratch_shapes=[pltpu.SemaphoreType.DMA((2, half, 2))] * 4
        + [pltpu.SemaphoreType.DMA((3,))],
        compiler_params=pltpu.CompilerParams(
            vmem_limit_bytes=32 * 1024 * 1024, collective_id=3, has_side_effects=True
        ),
        name="all_gather",
    )(x)
    return out.reshape((size * x.shape[0],) + x.shape[1:])


def subsample_kernel(
    size,
    x_ref,
    stem_ref,
    mid_dw_ref,
    mid_pw_ref,
    last_dw_ref,
    last_pw_ref,
    cot_ref,
    flat_ref,
    window_ref,
    even,
    odd,
    second,
    shifted,
    taps_ref,
    send,
    recv,
):
    exchange = Exchange(size, cot_ref, window_ref, send, recv)
    exchange.begin()
    rows = x_ref.shape[0] // 4
    main = rows - 8
    mids = second.shape[0] - 1
    span = shifted.shape[1] - 256
    odd[0] = jnp.zeros(odd.shape[1:], odd.dtype)
    second[0] = jnp.zeros(second.shape[1:], second.dtype)
    shifted[...] = jnp.zeros(shifted.shape, jnp.float32)
    for dt in range(3):
        for df in range(3):
            row = 3 * dt + df
            tap = stem_ref[dt, df : df + 1, :].astype(jnp.float32)
            for i in range(4):
                at = span + 2 * i + dt * MEL_PITCH + df
                shifted[i, at : at + 1, :] = tap
            taps_ref[row : row + 1, :] = mid_dw_ref[dt, df : df + 1, :].astype(jnp.float32)
            last = last_dw_ref[dt, df : df + 1, :].astype(jnp.float32)
            taps_ref[16 + row : 17 + row, :] = last

    def step(k, half):
        def stem(i):
            start = pl.multiple_of(span - 8 * k, 8)
            taps = shifted[i, pl.ds(start, 256), :].astype(jnp.bfloat16)
            return jnp.maximum(dot_nn(x_ref[...], taps), 0.0).reshape(even.shape)

        m = 2 * k + half
        even[...] = stem(2 * half)
        odd[1 - half] = stem(2 * half + 1)
        parts = (odd.at[half], even, odd.at[1 - half])
        early = jnp.zeros((main, 256), jnp.float32)
        late = jnp.zeros((rows, 256), jnp.float32)
        for df in range(3):
            src = parts[df]
            for dt in range(3):
                tap = taps_ref[3 * dt + df : 3 * dt + df + 1, :]
                phase = (3, 0, 1)[dt]
                start = 7 if dt == 0 else 8
                early += src[phase, start : start + main, :] * tap
                late += src[dt + 1] * tap
        weight = mid_pw_ref[...]
        second[m + 1, 0, 8:rows, :] = jnp.maximum(dot_nn(early.astype(jnp.bfloat16), weight), 0.0)
        second[m + 1, 1] = jnp.maximum(dot_nn(late.astype(jnp.bfloat16), weight), 0.0)

    def body(k, _):
        step(k, 0)
        step(k, 1)
        return 0

    lax.fori_loop(0, mids // 2, body, 0)
    exchange.forward()
    for f in range(mids // 2):
        total = jnp.zeros((main, 256), jnp.float32)
        for df in range(3):
            for dt in range(3):
                tap = taps_ref[16 + 3 * dt + df : 17 + 3 * dt + df, :]
                phase = (1, 0, 1)[dt]
                start = 7 if dt == 0 else 8
                total += second[2 * f + df, phase, start : start + main, :] * tap
        out = jnp.maximum(dot_nn(total.astype(jnp.bfloat16), last_pw_ref[...]), 0.0)
        flat_ref[:, f * 256 : (f + 1) * 256] = out.astype(jnp.bfloat16)
    exchange.finish()


def subsample(
    size,
    features,
    halo,
    stem_kernel,
    mid_depthwise,
    mid_pointwise,
    last_depthwise,
    last_pointwise,
    cotangent,
):
    feat_rows, mel = features.shape
    main = feat_rows // 8
    rows = main + 8
    channels = stem_kernel.shape[-1]
    mids = mel // 4
    blank = jnp.zeros((57, mel), features.dtype)
    series = jnp.concatenate([blank, halo, features, blank[:7]], axis=0)
    series = jnp.pad(series, ((0, 0), (1, MEL_PITCH - mel - 1)))
    eights = series.reshape(rows + 1, 8 * MEL_PITCH)
    wide = jnp.concatenate([eights[:-1], eights[1:, :MEL_PITCH]], axis=1)
    x = jnp.concatenate(
        [wide[:, 2 * p * MEL_PITCH : (2 * p + 3) * MEL_PITCH] for p in range(4)], axis=0
    )
    x = jnp.pad(x, ((0, 0), (0, 256 - 3 * MEL_PITCH)))
    return pl.pallas_call(
        functools.partial(subsample_kernel, size),
        out_shape=(
            jax.ShapeDtypeStruct((main, (mids // 2) * channels), jnp.bfloat16),
            jax.ShapeDtypeStruct((7,) + cotangent.shape, jnp.bfloat16),
        ),
        in_specs=[pl.BlockSpec(memory_space=pltpu.VMEM)] * 7,
        out_specs=(pl.BlockSpec(memory_space=pltpu.VMEM),) * 2,
        scratch_shapes=[
            pltpu.VMEM((4, rows, channels), jnp.float32),
            pltpu.VMEM((2, 4, rows, channels), jnp.float32),
            pltpu.VMEM((mids + 1, 2, rows, channels), jnp.float32),
            pltpu.VMEM((4, mel + 256, channels), jnp.float32),
            pltpu.VMEM((32, channels), jnp.float32),
        ]
        + EXCHANGE_SEMS,
        compiler_params=pltpu.CompilerParams(
            vmem_limit_bytes=40 * 1024 * 1024, collective_id=0, has_side_effects=True
        ),
        cost_estimate=pl.CostEstimate(
            flops=20_000_000_000, bytes_accessed=2_000_000, transcendentals=0
        ),
        name="subsample",
    )(
        x,
        stem_kernel,
        mid_depthwise,
        mid_pointwise,
        last_depthwise,
        last_pointwise,
        cotangent,
    )


def segments(positions, bounds_ref):
    found = jnp.zeros(positions.shape, jnp.int32)
    for u in range(bounds_ref.shape[0]):
        inside = (positions >= bounds_ref[u, 0]) & (positions < bounds_ref[u, 1])
        found = jnp.where(inside, u + 1, found)
    return found


def attention_kernel(
    size,
    proj_ref,
    do_ref,
    bounds_ref,
    live_ref,
    out_ref,
    grad_ref,
    bias_ref,
    bias2_ref,
    stat_ref,
    send,
    recv,
):
    rows = out_ref.shape[0]
    window = proj_ref.shape[0]
    width = out_ref.shape[1]
    own = slice(REACH * rows, (REACH + 1) * rows)
    me = lax.axis_index("tm")
    barrier = pltpu.get_barrier_semaphore()
    offsets = [o for o in range(-REACH, REACH + 1) if o]

    def when_there(offset, action):
        other = me + offset
        pl.when(jnp.logical_and(other >= 0, other < size))(lambda: action(offset))

    def greet(offset):
        pl.semaphore_signal(barrier, inc=1, device_id={"tm": me + offset}, device_id_type=MESH)

    def copy(offset):
        slot = REACH + offset
        return pltpu.make_async_remote_copy(
            src_ref=stat_ref.at[REACH],
            dst_ref=stat_ref.at[REACH - offset],
            send_sem=send.at[slot],
            recv_sem=recv.at[2 * REACH - slot],
            device_id={"tm": me + offset},
            device_id_type=MESH,
        )

    def incoming(offset):
        slot = REACH + offset
        return pltpu.make_async_remote_copy(
            src_ref=stat_ref.at[REACH],
            dst_ref=stat_ref.at[slot],
            send_sem=send.at[slot],
            recv_sem=recv.at[slot],
            device_id={"tm": me + offset},
            device_id_type=MESH,
        )

    for offset in offsets:
        when_there(offset, greet)

        @pl.when(jnp.logical_or(me + offset < 0, me + offset >= size))
        def _(offset=offset):
            stat_ref[REACH + offset] = jnp.zeros(stat_ref.shape[1:], jnp.float32)

    first = (me - REACH) * rows
    own_col = segments(me * rows + lax.broadcasted_iota(jnp.int32, (rows, 128), 0), bounds_ref)
    own_row = segments(me * rows + lax.broadcasted_iota(jnp.int32, (8, rows), 1), bounds_ref)[0:1]
    for b in range(2 * REACH + 1):
        place = first + b * rows
        live = live_ref[0, b] == 1
        col = segments(place + lax.broadcasted_iota(jnp.int32, (rows, 128), 0), bounds_ref)
        row = segments(place + lax.broadcasted_iota(jnp.int32, (8, rows), 1), bounds_ref)[0:1]
        span = slice(b * rows, (b + 1) * rows)
        bias_ref[span, :] = jnp.where((col[:, 0:1] == own_row) & live, 0.0, neg_fill)
        bias2_ref[:, span] = jnp.where((own_col[:, 0:1] == row) & live, 0.0, neg_fill)

    def column(group, h):
        return pl.ds(pl.multiple_of(group * width + h * HEAD_DIM, HEAD_DIM), HEAD_DIM)

    def forward(h):
        scores = dot_nt(proj_ref[:, column(1, h)], proj_ref[own, column(0, h)]) * SCALE
        scores = scores + bias_ref[...]
        top = jnp.max(scores, axis=0, keepdims=True)
        weights = jnp.exp(scores - top)
        total = jnp.sum(weights, axis=0, keepdims=True)
        probs = (weights * (1.0 / total)).astype(jnp.bfloat16)
        out = dot_tn(probs, proj_ref[:, column(2, h)])
        out_ref[:, column(0, h)] = out.astype(jnp.bfloat16)
        prod = do_ref[own, column(0, h)].astype(jnp.float32) * out
        stat_ref[REACH, h, 0:1, :] = top + jnp.log(total)
        stat_ref[REACH, h, 1:2, :] = jnp.sum(prod.T, axis=0, keepdims=True)

    def query_pass(h):
        keys = proj_ref[:, column(1, h)]
        scores = dot_nt(keys, proj_ref[own, column(0, h)]) * SCALE
        weights = jnp.exp(scores + bias_ref[...] - stat_ref[REACH, h, 0:1, :])
        dprob = dot_nt(proj_ref[:, column(2, h)], do_ref[own, column(0, h)])
        dscore = (weights * (dprob - stat_ref[REACH, h, 1:2, :])).astype(jnp.bfloat16)
        grad_ref[:, column(0, h)] = (dot_tn(dscore, keys) * SCALE).astype(jnp.bfloat16)

    def key_pass(h):
        queries = proj_ref[:, column(0, h)]
        douts = do_ref[:, column(0, h)]
        blocks = range(2 * REACH + 1)
        log_norms = jnp.concatenate([stat_ref[b, h, 0:1, :] for b in blocks], axis=1)
        deltas = jnp.concatenate([stat_ref[b, h, 1:2, :] for b in blocks], axis=1)
        scores = dot_nt(proj_ref[own, column(1, h)], queries) * SCALE
        weights = jnp.exp(scores + bias2_ref[...] - log_norms)
        dprob = dot_nt(proj_ref[own, column(2, h)], douts)
        dscore = (weights * (dprob - deltas)).astype(jnp.bfloat16)
        grad_ref[:, column(1, h)] = (dot_nn(dscore, queries) * SCALE).astype(jnp.bfloat16)
        grad_ref[:, column(2, h)] = dot_nn(weights.astype(jnp.bfloat16), douts).astype(jnp.bfloat16)

    def over_heads(work):
        def pair(i, _):
            work(2 * i)
            work(2 * i + 1)
            return 0

        lax.fori_loop(0, HEADS // 2, pair, 0)

    over_heads(forward)
    peers = 0
    for offset in offsets:
        peers += jnp.where(jnp.logical_and(me + offset >= 0, me + offset < size), 1, 0)
    pl.semaphore_wait(barrier, peers)
    for offset in offsets:
        when_there(offset, lambda o: copy(o).start())
    over_heads(query_pass)
    for offset in offsets:
        when_there(offset, lambda o: incoming(o).wait_recv())
    over_heads(key_pass)
    for offset in offsets:
        when_there(offset, lambda o: copy(o).wait_send())


def attention(size, projected, d_attention, utt_bounds, live_blocks):
    window = projected.shape[0]
    rows = window // (2 * REACH + 1)
    width = d_attention.shape[1]
    vmem = pl.BlockSpec(memory_space=pltpu.VMEM)
    smem = pl.BlockSpec(memory_space=pltpu.SMEM)
    return pl.pallas_call(
        functools.partial(attention_kernel, size),
        out_shape=(
            jax.ShapeDtypeStruct((rows, width), jnp.bfloat16),
            jax.ShapeDtypeStruct((rows, 3 * width), jnp.bfloat16),
        ),
        in_specs=[vmem, vmem, smem, smem],
        out_specs=(vmem, vmem),
        scratch_shapes=[
            pltpu.VMEM((window, rows), jnp.float32),
            pltpu.VMEM((rows, window), jnp.float32),
            pltpu.VMEM((2 * REACH + 1, HEADS, 2, rows), jnp.float32),
            pltpu.SemaphoreType.DMA((2 * REACH + 1,)),
            pltpu.SemaphoreType.DMA((2 * REACH + 1,)),
        ],
        compiler_params=pltpu.CompilerParams(
            vmem_limit_bytes=32 * 1024 * 1024, collective_id=2, has_side_effects=True
        ),
        cost_estimate=pl.CostEstimate(
            flops=20_000_000_000, bytes_accessed=8_000_000, transcendentals=2_000_000
        ),
        name="attention",
    )(projected, d_attention, utt_bounds, live_blocks)


def per_device(
    size,
    features,
    stem_kernel,
    mid_depthwise,
    mid_pointwise,
    last_depthwise,
    last_pointwise,
    proj_weight,
    norm_gain,
    qkv_weight,
    out_weight,
    cotangent,
    utt_bounds,
    live_blocks,
):
    halo = lax.ppermute(features[-8:], "tm", [(i, i + 1) for i in range(size - 1)])
    flat_rows, cot_window = subsample(
        size,
        features,
        halo,
        stem_kernel,
        mid_depthwise,
        mid_pointwise,
        last_depthwise,
        last_pointwise,
        cotangent,
    )
    cot_window = cot_window.reshape(-1, cotangent.shape[1])

    frames = dot_nn(flat_rows, proj_weight).astype(jnp.bfloat16)
    frames_f = frames.astype(jnp.float32)
    row_mean = jnp.mean(frames_f, axis=-1, keepdims=True)
    centered = frames_f - row_mean
    inv_std = lax.rsqrt(jnp.mean(centered * centered, axis=-1, keepdims=True) + norm_eps)
    normalized = centered * inv_std
    normed = (normalized * norm_gain).astype(jnp.bfloat16)
    normed_window = gathered_window(normed, size)
    normed_window, flat_sent, cot_window = lax.optimization_barrier(
        (normed_window, flat_rows, cot_window)
    )
    own_cols = size * (flat_rows.shape[1] // size)
    columns = lax.all_to_all(flat_sent[:, :own_cols], "tm", 1, 0, tiled=True)
    d_attention = dot_nt(cot_window, out_weight).astype(jnp.bfloat16)
    projected = dot_nn(normed_window, qkv_weight).astype(jnp.bfloat16)
    mixed, grads = attention(size, projected, d_attention, utt_bounds, live_blocks)
    grads, columns = lax.optimization_barrier((grads, columns))
    block_out = (frames_f + dot_nn(mixed, out_weight)).astype(jnp.bfloat16)
    grad_normed = dot_nt(grads, qkv_weight)
    scaled_grad = grad_normed * norm_gain
    ln_grad = inv_std * (
        scaled_grad
        - jnp.mean(scaled_grad, axis=-1, keepdims=True)
        - normalized * jnp.mean(scaled_grad * normalized, axis=-1, keepdims=True)
    )
    frame_grads = (cotangent.astype(jnp.float32) + ln_grad).astype(jnp.bfloat16)
    all_grads = gathered(frame_grads, size)
    proj_grads = dot_tn(columns, all_grads)
    return (block_out, frame_grads, proj_grads)


def solution(mesh):
    split = P(("groups", "tm"), None)
    in_specs = (split,) + (P(),) * 9 + (split, P("groups", None), split)
    return jax.shard_map(
        functools.partial(per_device, mesh.shape["tm"]),
        mesh=mesh,
        in_specs=in_specs,
        out_specs=(split, split, split),
        check_vma=False,
    )
```

```python
import functools

import jax
import jax.numpy as jnp
from jax import lax
from jax.experimental import pallas as pl
from jax.experimental.pallas import tpu as pltpu
from jax.sharding import PartitionSpec as P

HEADS = 8
REACH = 3
HEAD_DIM = 128
norm_eps = 1e-05
neg_fill = -1e30
MEL_PITCH = 84
SCALE = HEAD_DIM ** (-0.5)


def dot_nt(a, b):
    return lax.dot_general(a, b, (((1,), (1,)), ((), ())), preferred_element_type=jnp.float32)


def dot_tn(a, b):
    return lax.dot_general(a, b, (((0,), (0,)), ((), ())), preferred_element_type=jnp.float32)


def dot_nn(a, b):
    return jnp.dot(a, b, preferred_element_type=jnp.float32)


MESH = pl.DeviceIdType.MESH


class Exchange:
    def __init__(self, size, x_ref, out_ref, send, recv):
        self.size, self.x, self.out, self.send, self.recv = size, x_ref, out_ref, send, recv
        self.me = lax.axis_index("tm")
        self.odd = lax.rem(self.me, 2)
        self.sibling = self.me + 1 - 2 * self.odd
        self.far = self.me - 3 + 6 * self.odd
        self.has_low = self.me >= 2
        self.has_high = self.me + 2 < size
        self.has_far = jnp.logical_and(self.far >= 0, self.far < size)

    def copy(self, src, slot, sem, target):
        return pltpu.make_async_remote_copy(
            src_ref=src,
            dst_ref=self.out.at[slot],
            send_sem=self.send.at[sem],
            recv_sem=self.recv.at[sem],
            device_id={"tm": target},
            device_id_type=MESH,
        )

    def up(self):
        return self.copy(self.x, 1, 0, self.me + 2)

    def down(self):
        return self.copy(self.x, 5, 1, self.me - 2)

    def across(self):
        return self.copy(self.x, 2 + 2 * self.odd, 2, self.sibling)

    def remote(self):
        return self.copy(self.x, 6 - 6 * self.odd, 3, self.far)

    def pass_low(self):
        return self.copy(self.out.at[1], 2 * self.odd, 4, self.sibling)

    def pass_high(self):
        return self.copy(self.out.at[5], 4 + 2 * self.odd, 5, self.sibling)

    def local(self):
        return pltpu.make_async_copy(self.x, self.out.at[3], self.send.at[6])

    def begin(self):
        barrier = pltpu.get_barrier_semaphore()

        def greet(target):
            pl.semaphore_signal(barrier, inc=1, device_id={"tm": target}, device_id_type=MESH)

        greet(self.sibling)
        pl.when(self.has_low)(lambda: greet(self.me - 2))
        pl.when(self.has_high)(lambda: greet(self.me + 2))
        pl.when(self.has_far)(lambda: greet(self.far))
        self.local().start()
        for slot in range(7):
            if slot != 3:
                other = self.me + slot - 3
                outside = jnp.logical_or(other < 0, other >= self.size)

                @pl.when(outside)
                def _(slot=slot):
                    self.out[slot] = jnp.zeros(self.out.shape[1:], self.out.dtype)

        peers = 1
        for has in (self.has_low, self.has_high, self.has_far):
            peers += jnp.where(has, 1, 0)
        pl.semaphore_wait(barrier, peers)
        pl.when(self.has_high)(lambda: self.up().start())
        pl.when(self.has_low)(lambda: self.down().start())
        pl.when(self.has_far)(lambda: self.remote().start())
        self.across().start()

    def forward(self):
        @pl.when(self.has_low)
        def _():
            self.up().wait_recv()
            self.pass_low().start()

        @pl.when(self.has_high)
        def _():
            self.down().wait_recv()
            self.pass_high().start()

    def finish(self):
        self.local().wait()
        self.across().wait()
        pl.when(self.has_far)(lambda: self.remote().wait())

        @pl.when(self.has_low)
        def _():
            self.down().wait_send()
            self.pass_low().wait()

        @pl.when(self.has_high)
        def _():
            self.up().wait_send()
            self.pass_high().wait()


EXCHANGE_SEMS = [pltpu.SemaphoreType.DMA((7,)), pltpu.SemaphoreType.DMA((6,))]


def exchange_kernel(size, x_ref, cot_ref, weight_ref, out_ref, do_ref, send, recv):
    exchange = Exchange(size, x_ref, out_ref, send, recv)
    exchange.begin()
    do_ref[...] = dot_nt(cot_ref[...], weight_ref[...]).astype(jnp.bfloat16)
    exchange.forward()
    exchange.finish()


def gathered_window(x, cot_window, out_weight, size):
    out, d_attention = pl.pallas_call(
        functools.partial(exchange_kernel, size),
        out_shape=(
            jax.ShapeDtypeStruct((7,) + x.shape, x.dtype),
            jax.ShapeDtypeStruct(cot_window.shape, x.dtype),
        ),
        in_specs=[pl.BlockSpec(memory_space=pltpu.VMEM)] * 3,
        out_specs=(pl.BlockSpec(memory_space=pltpu.VMEM),) * 2,
        scratch_shapes=EXCHANGE_SEMS,
        compiler_params=pltpu.CompilerParams(
            vmem_limit_bytes=32 * 1024 * 1024, collective_id=1, has_side_effects=True
        ),
        name="exchange",
    )(x, cot_window, out_weight)
    return out.reshape((7 * x.shape[0],) + x.shape[1:]), d_attention


def gather_kernel(size, x_ref, out_ref, send, recv, side_send, side_recv, own_sem):
    chips = size // 2
    half = chips // 2
    rows = x_ref.shape[0]
    piece = rows // 2
    me = lax.axis_index("tm")
    core = lax.rem(me, 2)
    chip = me // 2
    sibling = me + 1 - 2 * core
    odd = lax.rem(chip, 2)
    place = jnp.where(odd == 0, chip // 2, chips - 1 - chip // 2)

    def device(offset):
        spot = lax.rem(place + offset + 2 * chips, chips)
        return jnp.where(spot < half, 2 * spot, 2 * (chips - 1 - spot) + 1) * 2 + core

    def remote(src, dst, send_sem, recv_sem, target):
        return pltpu.make_async_remote_copy(
            src_ref=src,
            dst_ref=dst,
            send_sem=send_sem,
            recv_sem=recv_sem,
            device_id={"tm": target},
            device_id_type=MESH,
        )

    def part(slot, c):
        return out_ref.at[slot, pl.ds(c * piece, piece), :]

    def along(way, k, c):
        sign = 1 - 2 * way
        slot = device(-sign * (k - 1))
        src = x_ref.at[pl.ds(c * piece, piece), :] if k == 1 else part(slot, c)
        index = (way, k - 1, c)
        return remote(src, part(slot, c), send.at[index], recv.at[index], device(sign))

    def arrived(way, k, c):
        sign = 1 - 2 * way
        slot = device(-sign * k)
        index = (way, k - 1, c)
        return remote(part(slot, c), part(slot, c), send.at[index], recv.at[index], device(sign))

    def side(way, k, c):
        slot = device(-(1 - 2 * way) * k)
        index = (way, k - 1, c)
        return remote(part(slot, c), part(slot, c), side_send.at[index], side_recv.at[index], sibling)

    def side_arrived(way, k, c):
        slot = device(-(1 - 2 * way) * k) + 1 - 2 * core
        index = (way, k - 1, c)
        return remote(part(slot, c), part(slot, c), side_send.at[index], side_recv.at[index], sibling)

    def used(way, k, c):
        return k < half or (k == half and c == way)

    steps = [
        (way, k, c)
        for k in range(1, half + 1)
        for c in range(2)
        for way in range(2)
        if used(way, k, c)
    ]
    barrier = pltpu.get_barrier_semaphore()
    for target in (device(1), device(-1), sibling):
        pl.semaphore_signal(barrier, inc=1, device_id={"tm": target}, device_id_type=MESH)
    own = pltpu.make_async_copy(x_ref, out_ref.at[me], own_sem.at[0])
    across = remote(x_ref, out_ref.at[me], own_sem.at[1], own_sem.at[2], sibling)
    own.start()
    pl.semaphore_wait(barrier, 3)
    for c in range(2):
        for way in range(2):
            along(way, 1, c).start()
    across.start()
    for way, k, c in steps:
        arrived(way, k, c).wait_recv()
        if used(way, k + 1, c):
            along(way, k + 1, c).start()
        side(way, k, c).start()
    own.wait()
    across.wait()
    for way, k, c in steps:
        side_arrived(way, k, c).wait_recv()
        side(way, k, c).wait_send()
        along(way, k, c).wait_send()


def gathered(x, size):
    half = size // 4
    out = pl.pallas_call(
        functools.partial(gather_kernel, size),
        out_shape=jax.ShapeDtypeStruct((size,) + x.shape, x.dtype),
        in_specs=[pl.BlockSpec(memory_space=pltpu.VMEM)],
        out_specs=pl.BlockSpec(memory_space=pltpu.VMEM),
        scratch_shapes=[pltpu.SemaphoreType.DMA((2, half, 2))] * 4
        + [pltpu.SemaphoreType.DMA((3,))],
        compiler_params=pltpu.CompilerParams(
            vmem_limit_bytes=32 * 1024 * 1024, collective_id=3, has_side_effects=True
        ),
        name="all_gather",
    )(x)
    return out.reshape((size * x.shape[0],) + x.shape[1:])


def subsample_kernel(
    size,
    x_ref,
    stem_ref,
    mid_dw_ref,
    mid_pw_ref,
    last_dw_ref,
    last_pw_ref,
    cot_ref,
    flat_ref,
    window_ref,
    even,
    odd,
    second,
    shifted,
    taps_ref,
    send,
    recv,
):
    exchange = Exchange(size, cot_ref, window_ref, send, recv)
    exchange.begin()
    rows = x_ref.shape[0] // 4
    main = rows - 8
    mids = second.shape[0] - 1
    span = shifted.shape[1] - 256
    odd[0] = jnp.zeros(odd.shape[1:], odd.dtype)
    second[0] = jnp.zeros(second.shape[1:], second.dtype)
    shifted[...] = jnp.zeros(shifted.shape, jnp.float32)
    for dt in range(3):
        for df in range(3):
            row = 3 * dt + df
            tap = stem_ref[dt, df : df + 1, :].astype(jnp.float32)
            for i in range(4):
                at = span + 2 * i + dt * MEL_PITCH + df
                shifted[i, at : at + 1, :] = tap
            taps_ref[row : row + 1, :] = mid_dw_ref[dt, df : df + 1, :].astype(jnp.float32)
            last = last_dw_ref[dt, df : df + 1, :].astype(jnp.float32)
            taps_ref[16 + row : 17 + row, :] = last

    def step(k, half):
        def stem(i):
            start = pl.multiple_of(span - 8 * k, 8)
            taps = shifted[i, pl.ds(start, 256), :].astype(jnp.bfloat16)
            return jnp.maximum(dot_nn(x_ref[...], taps), 0.0).reshape(even.shape)

        m = 2 * k + half
        even[...] = stem(2 * half)
        odd[1 - half] = stem(2 * half + 1)
        parts = (odd.at[half], even, odd.at[1 - half])
        early = jnp.zeros((main, 256), jnp.float32)
        late = jnp.zeros((rows, 256), jnp.float32)
        for df in range(3):
            src = parts[df]
            for dt in range(3):
                tap = taps_ref[3 * dt + df : 3 * dt + df + 1, :]
                phase = (3, 0, 1)[dt]
                start = 7 if dt == 0 else 8
                early += src[phase, start : start + main, :] * tap
                late += src[dt + 1] * tap
        weight = mid_pw_ref[...]
        second[m + 1, 0, 8:rows, :] = jnp.maximum(dot_nn(early.astype(jnp.bfloat16), weight), 0.0)
        second[m + 1, 1] = jnp.maximum(dot_nn(late.astype(jnp.bfloat16), weight), 0.0)

    def body(k, _):
        step(k, 0)
        step(k, 1)
        return 0

    lax.fori_loop(0, mids // 2, body, 0)
    exchange.forward()
    for f in range(mids // 2):
        total = jnp.zeros((main, 256), jnp.float32)
        for df in range(3):
            for dt in range(3):
                tap = taps_ref[16 + 3 * dt + df : 17 + 3 * dt + df, :]
                phase = (1, 0, 1)[dt]
                start = 7 if dt == 0 else 8
                total += second[2 * f + df, phase, start : start + main, :] * tap
        out = jnp.maximum(dot_nn(total.astype(jnp.bfloat16), last_pw_ref[...]), 0.0)
        flat_ref[:, f * 256 : (f + 1) * 256] = out.astype(jnp.bfloat16)
    exchange.finish()


def subsample(
    size,
    features,
    halo,
    stem_kernel,
    mid_depthwise,
    mid_pointwise,
    last_depthwise,
    last_pointwise,
    cotangent,
):
    feat_rows, mel = features.shape
    main = feat_rows // 8
    rows = main + 8
    channels = stem_kernel.shape[-1]
    mids = mel // 4
    blank = jnp.zeros((57, mel), features.dtype)
    series = jnp.concatenate([blank, halo, features, blank[:7]], axis=0)
    series = jnp.pad(series, ((0, 0), (1, MEL_PITCH - mel - 1)))
    eights = series.reshape(rows + 1, 8 * MEL_PITCH)
    wide = jnp.concatenate([eights[:-1], eights[1:, :MEL_PITCH]], axis=1)
    x = jnp.concatenate(
        [wide[:, 2 * p * MEL_PITCH : (2 * p + 3) * MEL_PITCH] for p in range(4)], axis=0
    )
    x = jnp.pad(x, ((0, 0), (0, 256 - 3 * MEL_PITCH)))
    return pl.pallas_call(
        functools.partial(subsample_kernel, size),
        out_shape=(
            jax.ShapeDtypeStruct((main, (mids // 2) * channels), jnp.bfloat16),
            jax.ShapeDtypeStruct((7,) + cotangent.shape, jnp.bfloat16),
        ),
        in_specs=[pl.BlockSpec(memory_space=pltpu.VMEM)] * 7,
        out_specs=(pl.BlockSpec(memory_space=pltpu.VMEM),) * 2,
        scratch_shapes=[
            pltpu.VMEM((4, rows, channels), jnp.float32),
            pltpu.VMEM((2, 4, rows, channels), jnp.float32),
            pltpu.VMEM((mids + 1, 2, rows, channels), jnp.float32),
            pltpu.VMEM((4, mel + 256, channels), jnp.float32),
            pltpu.VMEM((32, channels), jnp.float32),
        ]
        + EXCHANGE_SEMS,
        compiler_params=pltpu.CompilerParams(
            vmem_limit_bytes=40 * 1024 * 1024, collective_id=0, has_side_effects=True
        ),
        cost_estimate=pl.CostEstimate(
            flops=20_000_000_000, bytes_accessed=2_000_000, transcendentals=0
        ),
        name="subsample",
    )(
        x,
        stem_kernel,
        mid_depthwise,
        mid_pointwise,
        last_depthwise,
        last_pointwise,
        cotangent,
    )


def segments(positions, bounds_ref):
    found = jnp.zeros(positions.shape, jnp.int32)
    for u in range(bounds_ref.shape[0]):
        inside = (positions >= bounds_ref[u, 0]) & (positions < bounds_ref[u, 1])
        found = jnp.where(inside, u + 1, found)
    return found


def attention_kernel(
    size,
    proj_ref,
    do_ref,
    bounds_ref,
    live_ref,
    out_ref,
    grad_ref,
    bias_ref,
    bias2_ref,
    stat_ref,
    send,
    recv,
):
    rows = out_ref.shape[0]
    window = proj_ref.shape[0]
    width = out_ref.shape[1]
    own = slice(REACH * rows, (REACH + 1) * rows)
    me = lax.axis_index("tm")
    barrier = pltpu.get_barrier_semaphore()
    offsets = [o for o in range(-REACH, REACH + 1) if o]

    def when_there(offset, action):
        other = me + offset
        pl.when(jnp.logical_and(other >= 0, other < size))(lambda: action(offset))

    def greet(offset):
        pl.semaphore_signal(barrier, inc=1, device_id={"tm": me + offset}, device_id_type=MESH)

    def copy(offset):
        slot = REACH + offset
        return pltpu.make_async_remote_copy(
            src_ref=stat_ref.at[REACH],
            dst_ref=stat_ref.at[REACH - offset],
            send_sem=send.at[slot],
            recv_sem=recv.at[2 * REACH - slot],
            device_id={"tm": me + offset},
            device_id_type=MESH,
        )

    def incoming(offset):
        slot = REACH + offset
        return pltpu.make_async_remote_copy(
            src_ref=stat_ref.at[REACH],
            dst_ref=stat_ref.at[slot],
            send_sem=send.at[slot],
            recv_sem=recv.at[slot],
            device_id={"tm": me + offset},
            device_id_type=MESH,
        )

    for offset in offsets:
        when_there(offset, greet)

        @pl.when(jnp.logical_or(me + offset < 0, me + offset >= size))
        def _(offset=offset):
            stat_ref[REACH + offset] = jnp.zeros(stat_ref.shape[1:], jnp.float32)

    first = (me - REACH) * rows
    own_col = segments(me * rows + lax.broadcasted_iota(jnp.int32, (rows, 128), 0), bounds_ref)
    own_row = segments(me * rows + lax.broadcasted_iota(jnp.int32, (8, rows), 1), bounds_ref)[0:1]
    for b in range(2 * REACH + 1):
        place = first + b * rows
        live = live_ref[0, b] == 1
        col = segments(place + lax.broadcasted_iota(jnp.int32, (rows, 128), 0), bounds_ref)
        row = segments(place + lax.broadcasted_iota(jnp.int32, (8, rows), 1), bounds_ref)[0:1]
        span = slice(b * rows, (b + 1) * rows)
        bias_ref[span, :] = jnp.where((col[:, 0:1] == own_row) & live, 0.0, neg_fill)
        bias2_ref[:, span] = jnp.where((own_col[:, 0:1] == row) & live, 0.0, neg_fill)

    def column(group, h):
        return pl.ds(pl.multiple_of(group * width + h * HEAD_DIM, HEAD_DIM), HEAD_DIM)

    def forward(h):
        scores = dot_nt(proj_ref[:, column(1, h)], proj_ref[own, column(0, h)]) * SCALE
        scores = scores + bias_ref[...]
        top = jnp.max(scores, axis=0, keepdims=True)
        weights = jnp.exp(scores - top)
        total = jnp.sum(weights, axis=0, keepdims=True)
        probs = (weights * (1.0 / total)).astype(jnp.bfloat16)
        out = dot_tn(probs, proj_ref[:, column(2, h)])
        out_ref[:, column(0, h)] = out.astype(jnp.bfloat16)
        prod = do_ref[own, column(0, h)].astype(jnp.float32) * out
        stat_ref[REACH, h, 0:1, :] = top + jnp.log(total)
        stat_ref[REACH, h, 1:2, :] = jnp.sum(prod.T, axis=0, keepdims=True)

    def query_pass(h):
        keys = proj_ref[:, column(1, h)]
        scores = dot_nt(keys, proj_ref[own, column(0, h)]) * SCALE
        weights = jnp.exp(scores + bias_ref[...] - stat_ref[REACH, h, 0:1, :])
        dprob = dot_nt(proj_ref[:, column(2, h)], do_ref[own, column(0, h)])
        dscore = (weights * (dprob - stat_ref[REACH, h, 1:2, :])).astype(jnp.bfloat16)
        grad_ref[:, column(0, h)] = (dot_tn(dscore, keys) * SCALE).astype(jnp.bfloat16)

    def key_pass(h):
        queries = proj_ref[:, column(0, h)]
        douts = do_ref[:, column(0, h)]
        blocks = range(2 * REACH + 1)
        log_norms = jnp.concatenate([stat_ref[b, h, 0:1, :] for b in blocks], axis=1)
        deltas = jnp.concatenate([stat_ref[b, h, 1:2, :] for b in blocks], axis=1)
        scores = dot_nt(proj_ref[own, column(1, h)], queries) * SCALE
        weights = jnp.exp(scores + bias2_ref[...] - log_norms)
        dprob = dot_nt(proj_ref[own, column(2, h)], douts)
        dscore = (weights * (dprob - deltas)).astype(jnp.bfloat16)
        grad_ref[:, column(1, h)] = (dot_nn(dscore, queries) * SCALE).astype(jnp.bfloat16)
        grad_ref[:, column(2, h)] = dot_nn(weights.astype(jnp.bfloat16), douts).astype(jnp.bfloat16)

    def over_heads(work):
        def pair(i, _):
            work(2 * i)
            work(2 * i + 1)
            return 0

        lax.fori_loop(0, HEADS // 2, pair, 0)

    over_heads(forward)
    peers = 0
    for offset in offsets:
        peers += jnp.where(jnp.logical_and(me + offset >= 0, me + offset < size), 1, 0)
    pl.semaphore_wait(barrier, peers)
    for offset in offsets:
        when_there(offset, lambda o: copy(o).start())
    over_heads(query_pass)
    for offset in offsets:
        when_there(offset, lambda o: incoming(o).wait_recv())
    over_heads(key_pass)
    for offset in offsets:
        when_there(offset, lambda o: copy(o).wait_send())


def attention(size, projected, d_attention, utt_bounds, live_blocks):
    window = projected.shape[0]
    rows = window // (2 * REACH + 1)
    width = d_attention.shape[1]
    vmem = pl.BlockSpec(memory_space=pltpu.VMEM)
    smem = pl.BlockSpec(memory_space=pltpu.SMEM)
    return pl.pallas_call(
        functools.partial(attention_kernel, size),
        out_shape=(
            jax.ShapeDtypeStruct((rows, width), jnp.bfloat16),
            jax.ShapeDtypeStruct((rows, 3 * width), jnp.bfloat16),
        ),
        in_specs=[vmem, vmem, smem, smem],
        out_specs=(vmem, vmem),
        scratch_shapes=[
            pltpu.VMEM((window, rows), jnp.float32),
            pltpu.VMEM((rows, window), jnp.float32),
            pltpu.VMEM((2 * REACH + 1, HEADS, 2, rows), jnp.float32),
            pltpu.SemaphoreType.DMA((2 * REACH + 1,)),
            pltpu.SemaphoreType.DMA((2 * REACH + 1,)),
        ],
        compiler_params=pltpu.CompilerParams(
            vmem_limit_bytes=32 * 1024 * 1024, collective_id=2, has_side_effects=True
        ),
        cost_estimate=pl.CostEstimate(
            flops=20_000_000_000, bytes_accessed=8_000_000, transcendentals=2_000_000
        ),
        name="attention",
    )(projected, d_attention, utt_bounds, live_blocks)


def per_device(
    size,
    features,
    stem_kernel,
    mid_depthwise,
    mid_pointwise,
    last_depthwise,
    last_pointwise,
    proj_weight,
    norm_gain,
    qkv_weight,
    out_weight,
    cotangent,
    utt_bounds,
    live_blocks,
):
    halo = lax.ppermute(features[-8:], "tm", [(i, i + 1) for i in range(size - 1)])
    flat_rows, cot_window = subsample(
        size,
        features,
        halo,
        stem_kernel,
        mid_depthwise,
        mid_pointwise,
        last_depthwise,
        last_pointwise,
        cotangent,
    )
    cot_window = cot_window.reshape(-1, cotangent.shape[1])

    frames = dot_nn(flat_rows, proj_weight).astype(jnp.bfloat16)
    frames_f = frames.astype(jnp.float32)
    row_mean = jnp.mean(frames_f, axis=-1, keepdims=True)
    centered = frames_f - row_mean
    inv_std = lax.rsqrt(jnp.mean(centered * centered, axis=-1, keepdims=True) + norm_eps)
    normalized = centered * inv_std
    normed = (normalized * norm_gain).astype(jnp.bfloat16)
    normed_window, d_attention = gathered_window(normed, cot_window, out_weight, size)
    normed_window, flat_sent = lax.optimization_barrier((normed_window, flat_rows))
    own_cols = size * (flat_rows.shape[1] // size)
    columns = lax.all_to_all(flat_sent[:, :own_cols], "tm", 1, 0, tiled=True)
    projected = dot_nn(normed_window, qkv_weight).astype(jnp.bfloat16)
    mixed, grads = attention(size, projected, d_attention, utt_bounds, live_blocks)
    grads, columns = lax.optimization_barrier((grads, columns))
    block_out = (frames_f + dot_nn(mixed, out_weight)).astype(jnp.bfloat16)
    grad_normed = dot_nt(grads, qkv_weight)
    scaled_grad = grad_normed * norm_gain
    ln_grad = inv_std * (
        scaled_grad
        - jnp.mean(scaled_grad, axis=-1, keepdims=True)
        - normalized * jnp.mean(scaled_grad * normalized, axis=-1, keepdims=True)
    )
    frame_grads = (cotangent.astype(jnp.float32) + ln_grad).astype(jnp.bfloat16)
    all_grads = gathered(frame_grads, size)
    proj_grads = dot_tn(columns, all_grads)
    return (block_out, frame_grads, proj_grads)


def solution(mesh):
    split = P(("groups", "tm"), None)
    in_specs = (split,) + (P(),) * 9 + (split, P("groups", None), split)
    return jax.shard_map(
        functools.partial(per_device, mesh.shape["tm"]),
        mesh=mesh,
        in_specs=in_specs,
        out_specs=(split, split, split),
        check_vma=False,
    )
```
